32 devices in a mesh: parts: 2 (over y), dp: 4 (over x, core), tensor: 4 (over z).
Axes of the slice: x: 2, y: 2, z: 4, core: 2. Of those that a mesh axis runs over, the one named last changes fastest.
Arguments:
- tokens: bfloat16 [1024, 4096], P(('parts', 'dp')), parts along dimension 0, may hold values from -6 to 6
- cotangent: bfloat16 [1024, 4096], P(('parts', 'dp')), parts along dimension 0, may hold values from -6 to 6
- gate_blocks: bfloat16 [4, 112, 128, 128], P('tensor', 'dp'), may hold values from -0.25 to 0.25
- up_blocks: bfloat16 [4, 112, 128, 128], P('tensor', 'dp'), may hold values from -0.25 to 0.25
- down_blocks: bfloat16 [4, 112, 128, 128], P('tensor', 'dp'), may hold values from -0.125 to 0.125
- gate_index: int32 [2, 4, 112], P(None, 'tensor'), may hold values from 0 to 31, as said below
- up_index: int32 [2, 4, 112], P(None, 'tensor'), may hold values from 0 to 31, as said below
- down_index: int32 [2, 4, 112], P(None, 'tensor'), may hold values from 0 to 31, as said below
- block_counts: int32 [3, 4], P(None, 'tensor'), may hold values from 28 to 112, as said below
Outputs:
- layer_out: bfloat16 [1024, 4096], P(('parts', 'dp'), 'tensor'), parts along dimension 0
- token_grad: bfloat16 [1024, 4096], P(('parts', 'dp'), 'tensor'), parts along dimension 0
- gate_grad: bfloat16 [8, 112, 128, 128], P(('parts', 'tensor'), 'dp'), parts along dimension 0
- up_grad: bfloat16 [8, 112, 128, 128], P(('parts', 'tensor'), 'dp'), parts along dimension 0
- down_grad: bfloat16 [8, 112, 128, 128], P(('parts', 'tensor'), 'dp'), parts along dimension 0
The draws below stay inside these ranges and needn't reach their ends.
There are 2 independent parts, one for each index of `parts`. The reference program is written for one: setup_inputs(seed, part) draws one part's arguments, and reference() takes and returns one part's arrays. A program takes and returns all parts, laid end to end along the dimension named above; an argument that names none is the same for every part. Nothing has to cross between parts.
Inputs may be any that keep to these rules, and one draw needn't show every extreme that they name: `gate_index`: entry [0, r, s] is a feature block (below 32) and entry [1, r, s] a hidden block of group r (below 28); the 112 pairs of one group are distinct. `up_index`: as for gate_index. `down_index`: as for gate_index. `block_counts`: for each matrix some group uses all 112 slots.
All inputs are finite; a program needn't handle non-finite values.
Results may differ from the reference program's by a relative error of at most 0.0095.
Values may be sent and summed in bfloat16 or wider, within the bound.
No kernel may reach another device: no remote copies, remote signals or barrier semaphores. Data moves between devices by JAX's collectives and lax.ppermute only.
A program may use at most 128 MiB of HBM per device.

```python
import jax
import jax.numpy as jnp
from jax import lax

D = 4096
BLOCK = 128
TOK_DEV = 128
DB = 32
FB = 112
FBL = 28
CAP = 112
TOKENS = 512
N_DP = 4
N_TENSOR = 4


def draw_pairs(key):
    keys = jax.random.split(key, N_TENSOR)
    chosen = jax.vmap(lambda one_key: jax.random.permutation(one_key, DB * FBL)[:CAP])(keys)
    return jnp.stack([chosen // FBL, chosen % FBL]).astype(jnp.int32)


def draw_gate_index(key, part):
    return draw_pairs(jax.random.fold_in(key, 11))


def draw_up_index(key, part):
    return draw_pairs(jax.random.fold_in(key, 23))


def draw_down_index(key, part):
    return draw_pairs(jax.random.fold_in(key, 37))


def draw_block_counts(key, part):
    filled = jax.random.randint(jax.random.fold_in(key, 41), (3, N_TENSOR), max(CAP // 4, 1), CAP)
    busiest = jax.random.randint(jax.random.fold_in(key, 43), (3,), 0, N_TENSOR)
    chosen = jnp.arange(N_TENSOR, dtype=jnp.int32)[None, :] == busiest[:, None]
    return jnp.where(chosen, CAP, filled).astype(jnp.int32)


def block_scale(own_key, shape, pieces, low, high):
    factor_of = 1.0
    for position, shards_of in pieces:
        heights = jax.random.uniform(jax.random.fold_in(jax.random.fold_in(own_key, 6), position), (shards_of,), jnp.float32, low / len(pieces), high / len(pieces))
        factor_of = factor_of * jnp.repeat(jnp.exp(heights), shape[position] // shards_of).reshape((-1,) + (1,) * (len(shape) - 1 - position))
    return factor_of


def scatter_about(key, extent, spread, limit, cuts=(), held_as=jnp.bfloat16):
    array = spread * jax.random.normal(key, extent, jnp.float32)
    if cuts:
        array = array * block_scale(key, extent, cuts, -0.22, 0.18)
    return jnp.clip(array, -limit, limit).astype(held_as)


def setup_inputs(seed: int = 0, part: int = 0) -> dict:
    seeds = jax.random.split(jax.random.key(seed), 10)
    own_keys = jax.random.split(jax.random.fold_in(seeds[9], part), 10)
    tokens = scatter_about(own_keys[0], (TOKENS, D), 1.0, 6.0, ((0, 4),))
    cotangent = scatter_about(own_keys[1], (TOKENS, D), 1.0, 6.0, ((0, 4),))
    gate_blocks = scatter_about(seeds[2], (N_TENSOR, CAP, BLOCK, BLOCK), (BLOCK * DB // 8) ** -0.5, 0.25, ((0, 4), (1, 4)))
    up_blocks = scatter_about(seeds[3], (N_TENSOR, CAP, BLOCK, BLOCK), (BLOCK * DB // 8) ** -0.5, 0.25, ((0, 4), (1, 4)))
    down_blocks = scatter_about(seeds[4], (N_TENSOR, CAP, BLOCK, BLOCK), (BLOCK * FB // 8) ** -0.5, 0.125, ((0, 4), (1, 4)))
    gate_index = draw_gate_index(jax.random.fold_in(seeds[9], 71), part)
    up_index = draw_up_index(jax.random.fold_in(seeds[9], 71), part)
    down_index = draw_down_index(jax.random.fold_in(seeds[9], 71), part)
    block_counts = draw_block_counts(jax.random.fold_in(seeds[9], 71), part)
    return {"tokens": tokens, "cotangent": cotangent, "gate_blocks": gate_blocks, "up_blocks": up_blocks, "down_blocks": down_blocks, "gate_index": gate_index, "up_index": up_index, "down_index": down_index, "block_counts": block_counts}


PRECISE = lax.Precision.HIGHEST


def choose_blocks(source, positions, blocks_across):
    row_count = source.shape[0]
    lookup = (positions[:, None] == jnp.arange(blocks_across, dtype=jnp.int32)[None, :]).astype(jnp.float32)
    picked = jnp.einsum("tjc,kj->tkc", source.astype(jnp.float32).reshape(row_count, blocks_across, BLOCK), lookup, precision=PRECISE)
    return picked.astype(jnp.bfloat16)


def place_blocks(terms, positions, live_mask, blocks_across):
    row_count = terms.shape[0]
    masked = jnp.where(live_mask[None, :, None], terms, jnp.zeros_like(terms))
    placed = jnp.zeros((row_count, blocks_across, terms.shape[2]), terms.dtype).at[:, positions].add(masked)
    return placed.reshape(row_count, blocks_across * BLOCK)


def forward_product(picked, weights):
    return jnp.einsum("tkc,kcd->tkd", picked.astype(jnp.float32), weights, precision=PRECISE)


def backward_product(picked, weights):
    return jnp.einsum("tkd,kcd->tkc", picked.astype(jnp.float32), weights, precision=PRECISE)


def block_grads(left_pick, right_pick, live_mask):
    left_rows = left_pick.astype(jnp.float32).reshape(N_DP, TOK_DEV, CAP, BLOCK)
    right_rows = right_pick.astype(jnp.float32).reshape(N_DP, TOK_DEV, CAP, BLOCK)
    partial_sums = jnp.einsum("ptkc,ptkd->pkcd", left_rows, right_rows, precision=PRECISE)
    partial_sums = partial_sums * live_mask[None, :, None, None].astype(jnp.float32)
    rounded = lax.optimization_barrier(partial_sums.astype(jnp.bfloat16)).astype(jnp.float32)
    return jnp.sum(rounded, axis=0).astype(jnp.bfloat16)


def reference(tokens, cotangent, gate_blocks, up_blocks, down_blocks, gate_index, up_index, down_index, block_counts):
    slot_ids = jnp.arange(CAP, dtype=jnp.int32)

    def one_group(totals, group):
        out_total, grad_total = totals
        gate_weights = gate_blocks[group].astype(jnp.float32)
        up_weights = up_blocks[group].astype(jnp.float32)
        down_weights = down_blocks[group].astype(jnp.float32)
        gate_outer, gate_inner = gate_index[0, group], gate_index[1, group]
        up_outer, up_inner = up_index[0, group], up_index[1, group]
        down_outer, down_inner = down_index[0, group], down_index[1, group]
        gate_live = slot_ids < block_counts[0, group]
        up_live = slot_ids < block_counts[1, group]
        down_live = slot_ids < block_counts[2, group]
        tokens_gate = choose_blocks(tokens, gate_outer, DB)
        tokens_up = choose_blocks(tokens, up_outer, DB)
        gate_value = place_blocks(forward_product(tokens_gate, gate_weights), gate_inner, gate_live, FBL)
        up_value = place_blocks(forward_product(tokens_up, up_weights), up_inner, up_live, FBL)
        sigmoid_gate = jax.nn.sigmoid(gate_value)
        silu_gate = gate_value * sigmoid_gate
        hidden = (silu_gate * up_value).astype(jnp.bfloat16)
        hidden_down = choose_blocks(hidden, down_inner, FBL)
        out_part = place_blocks(forward_product(hidden_down, down_weights), down_outer, down_live, DB)
        out_total = out_total + lax.optimization_barrier(out_part.astype(jnp.bfloat16)).astype(jnp.float32)
        cot_down = choose_blocks(cotangent, down_outer, DB)
        hidden_grad = place_blocks(backward_product(cot_down, down_weights), down_inner, down_live, FBL)
        up_grad_value = (hidden_grad * silu_gate).astype(jnp.bfloat16)
        gate_grad_value = (hidden_grad * up_value * sigmoid_gate * (1.0 + gate_value * (1.0 - sigmoid_gate))).astype(jnp.bfloat16)
        pick_gate_grad = choose_blocks(gate_grad_value, gate_inner, FBL)
        pick_up_grad = choose_blocks(up_grad_value, up_inner, FBL)
        token_part = place_blocks(backward_product(pick_gate_grad, gate_weights), gate_outer, gate_live, DB)
        token_part = token_part + place_blocks(backward_product(pick_up_grad, up_weights), up_outer, up_live, DB)
        grad_total = grad_total + lax.optimization_barrier(token_part.astype(jnp.bfloat16)).astype(jnp.float32)
        gate_result = block_grads(tokens_gate, pick_gate_grad, gate_live)
        up_result = block_grads(tokens_up, pick_up_grad, up_live)
        down_result = block_grads(hidden_down, cot_down, down_live)
        return (out_total, grad_total), (gate_result, up_result, down_result)

    empty = jnp.zeros((TOKENS, D), jnp.float32)
    totals, grads = lax.scan(one_group, (empty, empty), jnp.arange(N_TENSOR, dtype=jnp.int32))
    return (totals[0].astype(jnp.bfloat16), totals[1].astype(jnp.bfloat16), grads[0], grads[1], grads[2])
```

```python
import functools

import jax
import jax.numpy as jnp
from jax import lax
from jax.experimental import pallas as pl
from jax.experimental.pallas import tpu as pltpu
from jax.sharding import PartitionSpec as P

FF = 14336
F32 = jnp.float32
BF16 = jnp.bfloat16
UNROLL = 4
NN = (((1,), (0,)), ((), ()))
NT = (((1,), (1,)), ((), ()))

VMEM = pl.BlockSpec(memory_space=pltpu.VMEM)
SMEM = pl.BlockSpec(memory_space=pltpu.SMEM)


def mm(left, right, dims=NN):
    return lax.dot_general(left, right, dims, preferred_element_type=F32)


def call(body, ints, arrays, outs, scratch=(), products=0, aliases=None):
    size = lambda a: a.size * a.dtype.itemsize
    total = sum(size(a) for a in arrays) + sum(size(o) for o in outs)
    held = total + sum(s.inner_aval.size * s.inner_aval.dtype.itemsize if hasattr(s, "inner_aval") else 0 for s in scratch)
    return pl.pallas_call(
        body,
        out_shape=outs,
        in_specs=[SMEM] * len(ints) + [VMEM] * len(arrays),
        out_specs=[VMEM] * len(outs),
        scratch_shapes=list(scratch),
        input_output_aliases=aliases or {},
        compiler_params=pltpu.CompilerParams(vmem_limit_bytes=held + (12 << 20)),
        cost_estimate=pl.CostEstimate(
            flops=products * 2 * 128**3 * 8, bytes_accessed=total, transcendentals=0
        ),
    )(*ints, *arrays)


class Place:
    def __init__(self, chips, parts, groups, shard):
        self.chips, self.parts, self.groups, self.shard = chips, parts, groups, shard

    def first(self, where, piece):
        chip, core, part = where[0], where[1], where[2]
        back, other, half = piece
        chip = lax.rem(chip + (self.chips - back), self.chips)
        core = 1 - core if other else core
        start = (chip * 2 + core) * self.shard
        if half is not None:
            start = start + (1 - part if half else part) * (self.shard // 2)
        return start


def over_live(live, terms, store):
    def several(step, _):
        slots = [step * UNROLL + u for u in range(UNROLL)]
        values = [terms(slot) for slot in slots]
        for slot, value in zip(slots, values):
            store(slot, value)
        return 0

    def single(slot, _):
        store(slot, terms(slot))
        return 0

    rounds = lax.div(live, UNROLL)
    lax.fori_loop(0, rounds, several, 0)
    lax.fori_loop(rounds * UNROLL, live, single, 0)


def live_in(count, first, extent):
    return jnp.clip(count - first, 0, extent)


def columns(block, size=128):
    return pl.ds(pl.multiple_of(block * size, size), size)


def zero(acc):
    acc[...] = jnp.zeros(acc.shape, acc.dtype)


def make(mesh):
    parts = mesh.shape["parts"]
    dp = mesh.shape["dp"]
    groups = mesh.shape["tensor"]
    chips = dp // 2

    def pair_swap(a):
        return lax.ppermute(a, "dp", [(i, i ^ 1) for i in range(dp)])

    def chip_shift(a, k):
        return lax.ppermute(
            a, "dp", [(i, ((i // 2 + k) % chips) * 2 + i % 2) for i in range(dp)]
        )

    def part_swap(a):
        return lax.ppermute(a, "parts", [(0, 1), (1, 0)])

    def group_shift(a, k):
        return lax.ppermute(a, "tensor", [(i, (i + k) % groups) for i in range(groups)])

    def per_device(
        tokens, cotangent, gate_blocks, up_blocks, down_blocks, gate_index, up_index, down_index, block_counts
    ):
        token_count, model_width = tokens.shape
        size = gate_blocks.shape[2]
        shard = gate_blocks.shape[1]
        model_blocks = model_width // size
        hidden_blocks = FF // size // groups
        halves = parts == 2 and shard % 2 == 0
        place = Place(chips, parts, groups, shard)
        at = lax.axis_index("dp")
        part = lax.axis_index("parts")
        where = jnp.stack([at // 2, at % 2, part, lax.axis_index("tensor")]).astype(jnp.int32)
        tables = [gate_index[:, 0], up_index[:, 0], down_index[:, 0]]
        counts = block_counts[:, 0]

        hidden_f32 = jax.ShapeDtypeStruct((hidden_blocks, token_count, size), F32)
        hidden_bf16 = jax.ShapeDtypeStruct((hidden_blocks, token_count, size), BF16)

        own = [gate_blocks[0], up_blocks[0], down_blocks[0]]
        keys = [(0, False, None), (0, True, None)]
        far_keys = []
        for k in range(1, chips):
            for half in (False, True) if halves else (None,):
                far_keys += [(k, False, half), (k, True, half)]
        sent = [
            lax.dynamic_slice_in_dim(w, part * (shard // 2), shard // 2, 0) if halves else w
            for w in own
        ]
        over_x = [[chip_shift(w, k) for k in range(1, chips)] for w in sent]
        near = [[w, pair_swap(w)] for w in own]
        far = []
        for arrived in over_x:
            pieces = []
            for w in arrived:
                pieces += [w, pair_swap(w)]
                if halves:
                    v = part_swap(w)
                    pieces += [v, pair_swap(v)]
            far.append(pieces)

        def turn(t_ref, o_ref):
            for j in range(model_blocks):
                o_ref[j] = t_ref[:, j * size : (j + 1) * size].T

        (tokens_t,) = call(
            turn, [], [tokens], [jax.ShapeDtypeStruct((model_blocks, size, token_count), BF16)]
        )
        tokens_t_pair = pair_swap(tokens_t)
        cotangent_pair = pair_swap(cotangent)

        def add_pieces(acc, x_ref, w_refs, piece_keys, table, count, where_ref):
            for w_ref, key in zip(w_refs, piece_keys):
                first = place.first(where_ref, key)

                def terms(s, w_ref=w_ref, first=first):
                    return mm(x_ref[:, columns(table[0, first + s])], w_ref[s])

                def store(s, value, first=first):
                    acc[table[1, first + s]] += value

                over_live(live_in(count, first, w_ref.shape[0]), terms, store)

        def near_body(where_ref, counts_ref, tg, tu, x_ref, g0, g1, u0, u1, acc_g, acc_u):
            zero(acc_g)
            zero(acc_u)
            add_pieces(acc_g, x_ref, [g0, g1], keys, tg, counts_ref[0], where_ref)
            add_pieces(acc_u, x_ref, [u0, u1], keys, tu, counts_ref[1], where_ref)

        acc_g, acc_u = call(
            near_body,
            [where, counts, tables[0], tables[1]],
            [tokens, *near[0], *near[1]],
            [hidden_f32, hidden_f32],
            products=4 * shard,
        )

        n_far = len(far_keys)

        def gate_body(where_ref, counts_ref, tg, acc_in, x_ref, *refs):
            w_refs, acc = refs[:n_far], refs[n_far]
            acc[...] = acc_in[...]
            add_pieces(acc, x_ref, w_refs, far_keys, tg, counts_ref[0], where_ref)

        (gate_value,) = call(
            gate_body,
            [where, counts, tables[0]],
            [acc_g, tokens, *far[0]],
            [hidden_f32],
            products=2 * shard,
        )

        def up_body(where_ref, counts_ref, tu, acc_in, gate_in, x_ref, *refs):
            w_refs = refs[:n_far]
            silu_ref, slope_ref, h_ref, ht_ref, acc = refs[n_far:]
            acc[...] = acc_in[...]
            add_pieces(acc, x_ref, w_refs, far_keys, tu, counts_ref[1], where_ref)

            def finish(b, _):
                gate, up = gate_in[b], acc[b]
                sigma = jax.nn.sigmoid(gate)
                silu = gate * sigma
                hidden = (silu * up).astype(BF16)
                silu_ref[b] = silu
                slope_ref[b] = up * sigma * (1.0 + gate * (1.0 - sigma))
                h_ref[b] = hidden
                ht_ref[b] = hidden.T
                return 0

            lax.fori_loop(0, hidden_blocks, finish, 0)

        silu, slope, hidden, hidden_t = call(
            up_body,
            [where, counts, tables[1]],
            [acc_u, gate_value, tokens, *far[1]],
            [
                hidden_f32,
                hidden_f32,
                hidden_bf16,
                jax.ShapeDtypeStruct((hidden_blocks, size, token_count), BF16),
            ],
            scratch=[pltpu.VMEM(hidden_f32.shape, F32)],
            products=2 * shard + 20,
        )
        hidden_t_pair = pair_swap(hidden_t)

        shard_out = jax.ShapeDtypeStruct((shard, size, size), BF16)

        def block_grads(m, ahead, left, right):
            def body(where_ref, counts_ref, table, l0, l1, r0, r1, *outs):
                for k, o_ref in zip(ahead, outs):
                    first = place.first(where_ref, ((chips - k) % chips, False, None))
                    live = live_in(counts_ref[m], first, shard)

                    def terms(s, first=first):
                        f, h = table[0, first + s], table[1, first + s]
                        if m == 2:
                            l, c = h, columns(f)
                            r = [r_ref[:, c] for r_ref in (r0, r1)]
                        else:
                            l = f
                            r = [r_ref[m, h] for r_ref in (r0, r1)]
                        return mm(
                            jnp.concatenate([l0[l], l1[l]], axis=1), jnp.concatenate(r, axis=0)
                        )

                    def store(s, value, o_ref=o_ref):
                        o_ref[s] = value.astype(BF16)

                    over_live(live, terms, store)

                    def clear(s, _, o_ref=o_ref):
                        o_ref[s] = jnp.zeros((size, size), BF16)
                        return 0

                    lax.fori_loop(live, shard, clear, 0)

            return call(
                body,
                [where, counts, tables[m]],
                [*left, *right],
                [shard_out] * len(ahead),
                products=len(ahead) * shard,
            )

        away = tuple(range(1, chips))

        def send(m, left, right):
            return [chip_shift(g, k) for g, k in zip(block_grads(m, away, left, right), away)]

        def total(kept, arrived):
            value = kept.astype(F32)
            for g in arrived:
                value = value + g.astype(F32)
            return value.astype(BF16)[None]

        down_operands = ([hidden_t, hidden_t_pair], [cotangent, cotangent_pair])
        down_far = send(2, *down_operands)

        def back_body(where_ref, counts_ref, td, c_ref, silu_ref, slope_ref, *refs):
            w_refs, o_ref, acc = refs[: 2 + n_far], refs[2 + n_far], refs[3 + n_far]
            zero(acc)
            for w_ref, key in zip(w_refs, keys + far_keys):
                first = place.first(where_ref, key)

                def terms(s, w_ref=w_ref, first=first):
                    return mm(c_ref[:, columns(td[0, first + s])], w_ref[s], NT)

                def store(s, value, first=first):
                    acc[td[1, first + s]] += value

                over_live(live_in(counts_ref[2], first, w_ref.shape[0]), terms, store)

            def finish(b, _):
                grad = acc[b]
                o_ref[0, b] = (grad * slope_ref[b]).astype(BF16)
                o_ref[1, b] = (grad * silu_ref[b]).astype(BF16)
                return 0

            lax.fori_loop(0, hidden_blocks, finish, 0)

        (grads,) = call(
            back_body,
            [where, counts, tables[2]],
            [cotangent, silu, slope, *near[2], *far[2]],
            [jax.ShapeDtypeStruct((2, hidden_blocks, token_count, size), BF16)],
            scratch=[pltpu.VMEM(hidden_f32.shape, F32)],
            products=4 * shard,
        )
        grads_pair = pair_swap(grads)
        token_operands = ([tokens_t, tokens_t_pair], [grads, grads_pair])
        gate_far = send(0, *token_operands)
        up_far = send(1, *token_operands)

        width = model_blocks // groups
        chunk = jax.ShapeDtypeStruct((token_count, width * size), BF16)

        def cut(where_ref, acc, outs):
            for k in range(groups):
                to = lax.rem(where_ref[3] + k, groups) * width
                for j in range(width):
                    outs[k][:, j * size : (j + 1) * size] = acc[to + j].astype(BF16)

        def out_body(where_ref, counts_ref, td, h_ref, *refs):
            w_refs, outs, acc = refs[: 2 + n_far], refs[2 + n_far : -1], refs[-1]
            zero(acc)
            for w_ref, key in zip(w_refs, keys + far_keys):
                first = place.first(where_ref, key)

                def terms(s, w_ref=w_ref, first=first):
                    return mm(h_ref[td[1, first + s]], w_ref[s])

                def store(s, value, first=first):
                    acc[td[0, first + s]] += value

                over_live(live_in(counts_ref[2], first, w_ref.shape[0]), terms, store)
            cut(where_ref, acc, outs)

        model_acc = pltpu.VMEM((model_blocks, token_count, size), F32)
        out_parts = call(
            out_body,
            [where, counts, tables[2]],
            [hidden, *near[2], *far[2]],
            [chunk] * groups,
            scratch=[model_acc],
            products=4 * shard,
        )

        def token_body(where_ref, counts_ref, tg, tu, y_ref, *refs):
            n = 2 + n_far
            outs, acc = refs[2 * n : -1], refs[-1]
            zero(acc)
            for m, table in ((0, tg), (1, tu)):
                for w_ref, key in zip(refs[m * n : (m + 1) * n], keys + far_keys):
                    first = place.first(where_ref, key)

                    def terms(s, m=m, table=table, w_ref=w_ref, first=first):
                        return mm(y_ref[m, table[1, first + s]], w_ref[s], NT)

                    def store(s, value, table=table, first=first):
                        acc[table[0, first + s]] += value

                    over_live(live_in(counts_ref[m], first, w_ref.shape[0]), terms, store)
            cut(where_ref, acc, outs)

        token_parts = call(
            token_body,
            [where, counts, tables[0], tables[1]],
            [grads, *near[0], *far[0], *near[1], *far[1]],
            [chunk] * groups,
            scratch=[model_acc],
            products=8 * shard,
        )

        def over_groups(chunks):
            value = chunks[0].astype(F32)
            for k in range(1, groups):
                value = value + group_shift(chunks[k], k).astype(F32)
            return value.astype(BF16)

        layer_out = over_groups(out_parts)
        token_grad = over_groups(token_parts)

        (down_kept,) = block_grads(2, (0,), *down_operands)
        (gate_kept,) = block_grads(0, (0,), *token_operands)
        (up_kept,) = block_grads(1, (0,), *token_operands)
        return (
            layer_out,
            token_grad,
            total(gate_kept, gate_far),
            total(up_kept, up_far),
            total(down_kept, down_far),
        )

    return per_device


def solution(mesh):
    return jax.shard_map(
        make(mesh),
        mesh=mesh,
        in_specs=(
            P(("parts", "dp"), None),
            P(("parts", "dp"), None),
            P("tensor", "dp", None, None),
            P("tensor", "dp", None, None),
            P("tensor", "dp", None, None),
            P(None, "tensor", None),
            P(None, "tensor", None),
            P(None, "tensor", None),
            P(None, "tensor"),
        ),
        out_specs=(
            P(("parts", "dp"), "tensor"),
            P(("parts", "dp"), "tensor"),
            P(("parts", "tensor"), "dp", None, None),
            P(("parts", "tensor"), "dp", None, None),
            P(("parts", "tensor"), "dp", None, None),
        ),
        check_vma=False,
    )
```

```python
import functools

import jax
import jax.numpy as jnp
from jax import lax
from jax.experimental import pallas as pl
from jax.experimental.pallas import tpu as pltpu
from jax.sharding import PartitionSpec as P

FF = 14336
F32 = jnp.float32
BF16 = jnp.bfloat16
UNROLL = 4
NN = (((1,), (0,)), ((), ()))
NT = (((1,), (1,)), ((), ()))
TN = (((0,), (0,)), ((), ()))

VMEM = pl.BlockSpec(memory_space=pltpu.VMEM)
SMEM = pl.BlockSpec(memory_space=pltpu.SMEM)


def mm(left, right, dims=NN):
    return lax.dot_general(left, right, dims, preferred_element_type=F32)


def call(body, ints, arrays, outs, scratch=(), products=0, aliases=None):
    size = lambda a: a.size * a.dtype.itemsize
    total = sum(size(a) for a in arrays) + sum(size(o) for o in outs)
    held = total + sum(s.inner_aval.size * s.inner_aval.dtype.itemsize if hasattr(s, "inner_aval") else 0 for s in scratch)
    return pl.pallas_call(
        body,
        out_shape=outs,
        in_specs=[SMEM] * len(ints) + [VMEM] * len(arrays),
        out_specs=[VMEM] * len(outs),
        scratch_shapes=list(scratch),
        input_output_aliases=aliases or {},
        compiler_params=pltpu.CompilerParams(vmem_limit_bytes=held + (12 << 20)),
        cost_estimate=pl.CostEstimate(
            flops=products, bytes_accessed=products, transcendentals=0
        ),
    )(*ints, *arrays)


class Place:
    def __init__(self, chips, parts, groups, shard):
        self.chips, self.parts, self.groups, self.shard = chips, parts, groups, shard

    def first(self, where, piece):
        chip, core, part = where[0], where[1], where[2]
        back, other, half = piece
        chip = lax.rem(chip + (self.chips - back), self.chips)
        core = 1 - core if other else core
        start = (chip * 2 + core) * self.shard
        if half is not None:
            start = start + (1 - part if half else part) * (self.shard // 2)
        return start


def over_live(live, terms, store):
    def several(step, _):
        slots = [step * UNROLL + u for u in range(UNROLL)]
        values = [terms(slot) for slot in slots]
        for slot, value in zip(slots, values):
            store(slot, value)
        return 0

    def single(slot, _):
        store(slot, terms(slot))
        return 0

    rounds = lax.div(live, UNROLL)
    lax.fori_loop(0, rounds, several, 0)
    lax.fori_loop(rounds * UNROLL, live, single, 0)


def live_in(count, first, extent):
    return jnp.clip(count - first, 0, extent)


def columns(block, size=128):
    return pl.ds(pl.multiple_of(block * size, size), size)


def after(value, *others):
    return lax.optimization_barrier((value, others))[0]


def zero(acc):
    acc[...] = jnp.zeros(acc.shape, acc.dtype)


def make(mesh):
    parts = mesh.shape["parts"]
    dp = mesh.shape["dp"]
    groups = mesh.shape["tensor"]
    chips = dp // 2

    def pair_swap(a, name):
        with jax.named_scope(name + "_core"):
            return lax.ppermute(a, "dp", [(i, i ^ 1) for i in range(dp)])

    def chip_shift(a, k, name):
        with jax.named_scope(name + "_chip"):
            return lax.ppermute(
                a, "dp", [(i, ((i // 2 + k) % chips) * 2 + i % 2) for i in range(dp)]
            )

    def part_swap(a, name):
        with jax.named_scope(name + "_part"):
            return lax.ppermute(a, "parts", [(0, 1), (1, 0)])

    def group_swap(a, bit, name):
        with jax.named_scope(name + "_group"):
            return lax.ppermute(a, "tensor", [(i, i ^ bit) for i in range(groups)])

    def per_device(
        tokens, cotangent, gate_blocks, up_blocks, down_blocks, gate_index, up_index, down_index, block_counts
    ):
        token_count, model_width = tokens.shape
        size = gate_blocks.shape[2]
        shard = gate_blocks.shape[1]
        model_blocks = model_width // size
        hidden_blocks = FF // size // groups
        halves = parts == 2 and shard % 2 == 0
        place = Place(chips, parts, groups, shard)
        at = lax.axis_index("dp")
        part = lax.axis_index("parts")
        where = jnp.stack([at // 2, at % 2, part, lax.axis_index("tensor")]).astype(jnp.int32)
        tables = [gate_index[:, 0], up_index[:, 0], down_index[:, 0]]
        counts = block_counts[:, 0]

        hidden_f32 = jax.ShapeDtypeStruct((hidden_blocks, token_count, size), F32)
        hidden_bf16 = jax.ShapeDtypeStruct((hidden_blocks, token_count, size), BF16)

        own = [gate_blocks[0], up_blocks[0], down_blocks[0]]
        near_keys = [(0, False, None), (0, True, None)]
        away = tuple(range(1, chips))
        near_half, far_half = (False, True) if halves else (None, None)
        direct_keys = [(k, other, near_half) for k in away for other in (False, True)]
        relay_keys = [(k, other, far_half) for k in away for other in (False, True)] if halves else []
        all_keys = near_keys + direct_keys + relay_keys
        cut = own
        if halves:
            cut = [
                lax.dynamic_slice_in_dim(w, part * (shard // 2), shard // 2, 0) for w in own
            ]

        def shift_all(name, blocks, *others):
            arrived = []
            for k in away:
                arrived.append(chip_shift(after(blocks, *others), k, name))
                others = arrived[-1:]
            return arrived

        names = ("gate", "up", "down")
        near = [[w, pair_swap(w, name)] for w, name in zip(own[:2], names)]

        def both(name, pieces):
            return [q for w in pieces for q in (w, pair_swap(w, name))]

        def add_pieces(acc, m, x_ref, w_refs, piece_keys, table, counts_ref, where_ref):
            for w_ref, key in zip(w_refs, piece_keys):
                first = place.first(where_ref, key)

                def terms(s, w_ref=w_ref, first=first):
                    return mm(x_ref[:, columns(table[0, first + s])], w_ref[s], NT if m == 2 else NN)

                def store(s, value, first=first):
                    acc[table[1, first + s]] += value

                over_live(live_in(counts_ref[m], first, w_ref.shape[0]), terms, store)

        def begin(m, x, pieces, piece_keys):
            def body(where_ref, counts_ref, table, x_ref, *refs):
                zero(refs[-1])
                add_pieces(refs[-1], m, x_ref, refs[:-1], piece_keys, table, counts_ref, where_ref)

            (acc,) = call(
                body, [where, counts, tables[m]], [x, *pieces], [hidden_f32],
                products=sum(p.shape[0] for p in pieces),
            )
            return acc

        def go_on(m, acc, x, pieces, piece_keys):
            if not pieces:
                return acc

            def body(where_ref, counts_ref, table, acc_in, x_ref, *refs):
                add_pieces(refs[-1], m, x_ref, refs[:-1], piece_keys, table, counts_ref, where_ref)

            (acc,) = call(
                body, [where, counts, tables[m]], [acc, x, *pieces], [hidden_f32],
                products=sum(p.shape[0] for p in pieces), aliases={3: 0},
            )
            return acc

        def relayed(name, pieces, *others):
            out = []
            for w in pieces if halves else []:
                out.append(part_swap(after(w, *others), name))
                others = out[-1:]
            return out

        acc_g = begin(0, tokens, near[0], near_keys)
        acc_u = begin(1, tokens, near[1], near_keys)
        tokens_pair = pair_swap(tokens, "tokens")
        cotangent_pair = pair_swap(cotangent, "cotangent")

        x_g = shift_all("gate", cut[0])
        x_g = after(x_g, acc_g, tokens_pair, cotangent_pair)
        x_u = shift_all("up", cut[1], *x_g)
        y_g = relayed("gate", x_g)

        near.append([own[2], pair_swap(after(own[2], *x_g), "down")])
        direct = [both("gate_x", after(x_g, acc_u))]
        x_u, y_g = after((x_u, y_g), acc_u)
        x_d = shift_all("down", cut[2], *x_u)
        acc_g = go_on(0, after(acc_g, *x_u), tokens, direct[0], direct_keys)
        y_u = relayed("up", x_u)
        direct.append(both("up_x", after(x_u, acc_g)))
        acc_h = begin(2, cotangent, near[2], near_keys)
        relay = [both("gate_y", after(y_g, acc_g))]

        acc_u = go_on(1, acc_u, tokens, direct[1], direct_keys)

        def gate_body(where_ref, counts_ref, tg, acc_in, x_ref, *refs):
            w_refs, silu_ref, slope_ref, acc = refs[:-3], *refs[-3:]
            acc[...] = acc_in[...]
            add_pieces(acc, 0, x_ref, w_refs, relay_keys, tg, counts_ref, where_ref)

            def finish(b, _):
                gate = acc[b]
                sigma = jax.nn.sigmoid(gate)
                silu_ref[b] = gate * sigma
                slope_ref[b] = sigma * (1.0 + gate * (1.0 - sigma))
                return 0

            lax.fori_loop(0, hidden_blocks, finish, 0)

        silu, slope = call(
            gate_body,
            [where, counts, tables[0]],
            [acc_g, tokens, *relay[0]],
            [hidden_f32, hidden_f32],
            scratch=[pltpu.VMEM(hidden_f32.shape, F32)],
            products=shard,
        )
        x_d = after(x_d, acc_u, silu, acc_h)
        y_u = after(y_u, *x_d)
        y_d = relayed("down", x_d, *y_u)
        direct.append(both("down_x", x_d))
        relay.append(both("up_y", y_u))

        quarter = token_count // 4

        def up_body(where_ref, counts_ref, tu, acc_in, silu_ref, x_ref, *refs):
            w_refs, acc, h_refs = refs[:-5], refs[-5], refs[-4:]
            add_pieces(acc, 1, x_ref, w_refs, relay_keys, tu, counts_ref, where_ref)

            def finish(b, _):
                hidden = (silu_ref[b] * acc[b]).astype(BF16)
                for i, h_ref in enumerate(h_refs):
                    h_ref[b] = hidden[i * quarter : (i + 1) * quarter]
                return 0

            lax.fori_loop(0, hidden_blocks, finish, 0)

        up_value, *hidden = call(
            up_body,
            [where, counts, tables[1]],
            [acc_u, silu, tokens, *relay[1]],
            [
                hidden_f32,
                *[jax.ShapeDtypeStruct((hidden_blocks, quarter, size), BF16)] * 4,
            ],
            aliases={3: 0},
            products=shard + 20,
        )
        hidden_pair = after([pair_swap(h, "hidden") for h in hidden], *y_d)

        def block_grads(m, ahead, left, right, cuts=(0, shard)):
            spans = [(k, low, high) for k in ahead for low, high in zip(cuts, cuts[1:])]

            n_left, n_both = len(left), len(left) + len(right)

            def body(where_ref, counts_ref, table, *refs):
                ls, rs, outs = refs[:n_left], refs[n_left:n_both], refs[n_both:]
                for (k, low, high), o_ref in zip(spans, outs):
                    first = place.first(where_ref, ((chips - k) % chips, False, None)) + low
                    live = live_in(counts_ref[m], first, high - low)

                    def terms(s, first=first):
                        f, h = table[0, first + s], table[1, first + s]
                        wide, deep = (rs, ls) if m == 2 else (ls, rs)
                        model = jnp.concatenate([ref[:, columns(f)] for ref in wide], axis=0)
                        inner = jnp.concatenate([ref[h] for ref in deep], axis=0)
                        return mm(inner, model, TN) if m == 2 else mm(model, inner, TN)

                    def store(s, value, o_ref=o_ref):
                        o_ref[s] = value.astype(BF16)

                    over_live(live, terms, store)

                    def clear(s, _, o_ref=o_ref):
                        o_ref[s] = jnp.zeros((size, size), BF16)
                        return 0

                    lax.fori_loop(live, high - low, clear, 0)

            return call(
                body,
                [where, counts, tables[m]],
                [*left, *right],
                [jax.ShapeDtypeStruct((high - low, size, size), BF16) for _, low, high in spans],
                products=len(ahead) * shard,
            )

        def total(kept, arrived):
            value = kept.astype(F32)
            for g in arrived:
                value = value + g.astype(F32)
            return value.astype(BF16)[None]

        down_operands = ([*hidden, *hidden_pair], [cotangent, cotangent_pair])
        cuts = tuple(sorted({0, max(shard // 4, 1), shard}))
        down_away = [block_grads(2, away, *down_operands, cuts=cuts[:2])]
        held = [*after(hidden, *down_away[0]), *hidden_pair]
        rest = block_grads(2, away, held, down_operands[1], cuts=cuts[1:])
        steps = len(cuts) - 2
        down_away += [rest[i::steps] for i in range(steps)]
        hurry = [g for grads in down_away[1:] for g in grads]
        down_far = []
        for grads in down_away:
            grads = after(grads, *(down_far[-1] if down_far else []))
            down_far.append([chip_shift(g, k, "down_grad") for g, k in zip(grads, away)])
            if hurry:
                down_far[0], hurry = after(down_far[0], *hurry), []
        down_lead, down_last = down_far[0], down_far[-1]

        relay.append(both("down_y", after(y_d, *down_lead)))
        acc_h = go_on(2, after(acc_h, *down_lead), cotangent, direct[2], direct_keys)

        half_tokens = token_count // 2

        def back_body(where_ref, counts_ref, td, acc_in, c_ref, silu_ref, slope_ref, up_ref, *refs):
            outs, acc = refs[-4:-1], refs[-1]
            acc[...] = acc_in[...]
            add_pieces(acc, 2, c_ref, refs[:-4], relay_keys, td, counts_ref, where_ref)

            def finish(b, _):
                grad = acc[b]
                gate = (grad * up_ref[b] * slope_ref[b]).astype(BF16)
                up = (grad * silu_ref[b]).astype(BF16)
                for i in range(2):
                    rows = slice(i * half_tokens, (i + 1) * half_tokens)
                    outs[i][b] = gate[rows]
                outs[2][b] = up
                return 0

            lax.fori_loop(0, hidden_blocks, finish, 0)

        grads = call(
            back_body,
            [where, counts, tables[2]],
            [acc_h, cotangent, silu, slope, up_value, *relay[2]],
            [jax.ShapeDtypeStruct((hidden_blocks, half_tokens, size), BF16)] * 2 + [hidden_bf16],
            scratch=[pltpu.VMEM(hidden_f32.shape, F32)],
            products=shard + 10,
        )
        pieces = [near[m] + direct[m] + relay[m] for m in range(3)]

        width = model_blocks // groups
        chunk = jax.ShapeDtypeStruct((groups // 2, token_count, width * size), BF16)

        def deal(where_ref, acc, outs):
            for i in range(groups):
                to = lax.bitwise_xor(where_ref[3], i) * width
                for j in range(width):
                    outs[i % 2][i // 2, :, j * size : (j + 1) * size] = acc[to + j].astype(BF16)

        def out_body(where_ref, counts_ref, td, *refs):
            h_refs, refs = refs[:4], refs[4:]
            w_refs, outs, acc = refs[: len(all_keys)], refs[len(all_keys) : -1], refs[-1]
            zero(acc)
            for w_ref, key in zip(w_refs, all_keys):
                first = place.first(where_ref, key)

                def terms(s, w_ref=w_ref, first=first):
                    h = td[1, first + s]
                    return mm(jnp.concatenate([h_ref[h] for h_ref in h_refs], axis=0), w_ref[s])

                def store(s, value, first=first):
                    acc[td[0, first + s]] += value

                over_live(live_in(counts_ref[2], first, w_ref.shape[0]), terms, store)
            deal(where_ref, acc, outs)

        model_acc = pltpu.VMEM((model_blocks, token_count, size), F32)
        out_parts = call(
            out_body,
            [where, counts, tables[2]],
            [*after(hidden, *grads), *pieces[2]],
            [chunk] * 2,
            scratch=[model_acc],
            products=4 * shard,
        )

        grads_pair = [pair_swap(g, "grads") for g in grads]
        grads_pair[:2] = after(grads_pair[:2], *out_parts)
        gate_operands = ([tokens, tokens_pair], [*grads[:2], *grads_pair[:2]])
        up_operands = ([tokens, tokens_pair], [grads[2], after(grads_pair[2], *down_last)])
        gate_away = block_grads(0, away, *gate_operands)

        def token_body(where_ref, counts_ref, tg, tu, *refs):
            ys, refs = refs[:3], refs[3:]
            n = len(all_keys)
            outs, acc = refs[2 * n : -1], refs[-1]
            zero(acc)
            for m, table in ((0, tg), (1, tu)):
                for w_ref, key in zip(refs[m * n : (m + 1) * n], all_keys):
                    first = place.first(where_ref, key)

                    def terms(s, m=m, table=table, w_ref=w_ref, first=first):
                        h = table[1, first + s]
                        y = ys[2][h] if m else jnp.concatenate([ys[0][h], ys[1][h]], axis=0)
                        return mm(y, w_ref[s], NT)

                    def store(s, value, table=table, first=first):
                        acc[table[0, first + s]] += value

                    over_live(live_in(counts_ref[m], first, w_ref.shape[0]), terms, store)
            deal(where_ref, acc, outs)

        token_parts = call(
            token_body,
            [where, counts, tables[0], tables[1]],
            [*after(grads, *gate_away), *pieces[0], *pieces[1]],
            [chunk] * 2,
            scratch=[model_acc],
            products=8 * shard,
        )

        def swap_groups(name, chunks, *others):
            kept, sent = chunks
            bit, first = 1, None
            while True:
                arrived = group_swap(sent, bit, name)
                first = arrived if first is None else first
                bit *= 2
                if bit == groups:
                    return first, kept, arrived
                value = (kept.astype(F32) + after(arrived, *others).astype(F32)).astype(BF16)
                kept, sent = value[0::2], value[1::2]

        def last_sum(kept, arrived, *others):
            value = kept.astype(F32) + after(arrived, *others).astype(F32)
            return value[0].astype(BF16)

        up_away = block_grads(1, away, *up_operands)
        down_last = down_far[-1] = after(down_last, *gate_away)
        gate_far = [chip_shift(g, k, "gate_grad") for g, k in zip(after(gate_away, *down_last), away)]
        kept_t, kept_h = after((tokens, hidden), *down_last)
        (down_kept,) = block_grads(2, (0,), [*kept_h, *hidden_pair], down_operands[1])
        (gate_kept,) = block_grads(0, (0,), [kept_t, tokens_pair], gate_operands[1])
        (up_kept,) = block_grads(1, (0,), [kept_t, tokens_pair], up_operands[1])
        joined = [jnp.concatenate(steps, axis=0) for steps in zip(*down_far)]
        down_grad = total(down_kept, joined)
        out_first, *out_terms = swap_groups("out", out_parts, *token_parts)
        gate_far = after(gate_far, down_grad, gate_kept, up_kept, out_first, *up_away)
        up_far = [chip_shift(g, k, "up_grad") for g, k in zip(after(up_away, *gate_far), away)]
        gate_grad = total(gate_kept, gate_far)
        layer_out = last_sum(*out_terms, gate_grad)
        _, *token_terms = swap_groups("token", token_parts, gate_grad)
        token_grad = last_sum(*token_terms, layer_out)
        up_grad = total(up_kept, after(up_far, token_grad))
        return layer_out, token_grad, gate_grad, up_grad, down_grad

    return per_device


def solution(mesh):
    return jax.shard_map(
        make(mesh),
        mesh=mesh,
        in_specs=(
            P(("parts", "dp"), None),
            P(("parts", "dp"), None),
            P("tensor", "dp", None, None),
            P("tensor", "dp", None, None),
            P("tensor", "dp", None, None),
            P(None, "tensor", None),
            P(None, "tensor", None),
            P(None, "tensor", None),
            P(None, "tensor"),
        ),
        out_specs=(
            P(("parts", "dp"), "tensor"),
            P(("parts", "dp"), "tensor"),
            P(("parts", "tensor"), "dp", None, None),
            P(("parts", "tensor"), "dp", None, None),
            P(("parts", "tensor"), "dp", None, None),
        ),
        check_vma=False,
    )
```

```python
import functools

import jax
import jax.numpy as jnp
from jax import lax
from jax.experimental import pallas as pl
from jax.experimental.pallas import tpu as pltpu
from jax.sharding import PartitionSpec as P

FF = 14336
F32 = jnp.float32
BF16 = jnp.bfloat16
UNROLL = 4
NN = (((1,), (0,)), ((), ()))
NT = (((1,), (1,)), ((), ()))
TN = (((0,), (0,)), ((), ()))

VMEM = pl.BlockSpec(memory_space=pltpu.VMEM)
SMEM = pl.BlockSpec(memory_space=pltpu.SMEM)


def mm(left, right, dims=NN):
    return lax.dot_general(left, right, dims, preferred_element_type=F32)


def call(body, ints, arrays, outs, scratch=(), products=0, aliases=None):
    size = lambda a: a.size * a.dtype.itemsize
    total = sum(size(a) for a in arrays) + sum(size(o) for o in outs)
    held = total + sum(s.inner_aval.size * s.inner_aval.dtype.itemsize if hasattr(s, "inner_aval") else 0 for s in scratch)
    return pl.pallas_call(
        body,
        out_shape=outs,
        in_specs=[SMEM] * len(ints) + [VMEM] * len(arrays),
        out_specs=[VMEM] * len(outs),
        scratch_shapes=list(scratch),
        input_output_aliases=aliases or {},
        compiler_params=pltpu.CompilerParams(vmem_limit_bytes=held + (12 << 20)),
        cost_estimate=pl.CostEstimate(
            flops=products, bytes_accessed=products, transcendentals=0
        ),
    )(*ints, *arrays)


class Place:
    def __init__(self, chips, parts, groups, shard):
        self.chips, self.parts, self.groups, self.shard = chips, parts, groups, shard

    def first(self, where, piece):
        chip, core, part = where[0], where[1], where[2]
        back, other, half, offset = piece
        chip = lax.rem(chip + (self.chips - back), self.chips)
        core = 1 - core if other else core
        start = (chip * 2 + core) * self.shard
        if half is not None:
            start = start + (1 - part if half else part) * (self.shard // 2)
        return start + offset


def over_live(live, terms, store):
    def several(step, _):
        slots = [step * UNROLL + u for u in range(UNROLL)]
        values = [terms(slot) for slot in slots]
        for slot, value in zip(slots, values):
            store(slot, value)
        return 0

    def single(slot, _):
        store(slot, terms(slot))
        return 0

    rounds = lax.div(live, UNROLL)
    lax.fori_loop(0, rounds, several, 0)
    lax.fori_loop(rounds * UNROLL, live, single, 0)


def live_in(count, first, extent):
    return jnp.clip(count - first, 0, extent)


def columns(block, size=128):
    return pl.ds(pl.multiple_of(block * size, size), size)


def after(value, *others):
    return lax.optimization_barrier((value, others))[0]


def zero(acc):
    acc[...] = jnp.zeros(acc.shape, acc.dtype)


def make(mesh):
    parts = mesh.shape["parts"]
    dp = mesh.shape["dp"]
    groups = mesh.shape["tensor"]
    chips = dp // 2

    def pair_swap(a, name):
        with jax.named_scope(name + "_core"):
            return lax.ppermute(a, "dp", [(i, i ^ 1) for i in range(dp)])

    def chip_shift(a, k, name):
        with jax.named_scope(name + "_chip"):
            return lax.ppermute(
                a, "dp", [(i, ((i // 2 + k) % chips) * 2 + i % 2) for i in range(dp)]
            )

    def part_swap(a, name):
        with jax.named_scope(name + "_part"):
            return lax.ppermute(a, "parts", [(0, 1), (1, 0)])

    def group_swap(a, bit, name):
        with jax.named_scope(name + "_group"):
            return lax.ppermute(a, "tensor", [(i, i ^ bit) for i in range(groups)])

    def per_device(
        tokens, cotangent, gate_blocks, up_blocks, down_blocks, gate_index, up_index, down_index, block_counts
    ):
        token_count, model_width = tokens.shape
        size = gate_blocks.shape[2]
        shard = gate_blocks.shape[1]
        model_blocks = model_width // size
        hidden_blocks = FF // size // groups
        halves = parts == 2 and shard % 2 == 0
        place = Place(chips, parts, groups, shard)
        at = lax.axis_index("dp")
        part = lax.axis_index("parts")
        where = jnp.stack([at // 2, at % 2, part, lax.axis_index("tensor")]).astype(jnp.int32)
        tables = [gate_index[:, 0], up_index[:, 0], down_index[:, 0]]
        counts = block_counts[:, 0]

        hidden_f32 = jax.ShapeDtypeStruct((hidden_blocks, token_count, size), F32)
        hidden_bf16 = jax.ShapeDtypeStruct((hidden_blocks, token_count, size), BF16)

        own = [gate_blocks[0], up_blocks[0], down_blocks[0]]
        near_keys = [(0, False, None, 0), (0, True, None, 0)]
        away = tuple(range(1, chips))
        near_half, far_half = (False, True) if halves else (None, None)
        direct_keys = [(k, other, near_half, 0) for k in away for other in (False, True)]
        relay_keys = [(k, other, far_half, 0) for k in away for other in (False, True)] if halves else []
        every = near_keys + direct_keys + relay_keys
        all_keys = [every, every, every]
        cut = own
        if halves:
            cut = [
                lax.dynamic_slice_in_dim(w, part * (shard // 2), shard // 2, 0) for w in own
            ]

        def shift_all(name, blocks, *others):
            arrived = []
            for k in away:
                arrived.append(chip_shift(after(blocks, *others), k, name))
                others = arrived[-1:]
            return arrived

        names = ("gate", "up", "down")
        near = [[w, pair_swap(w, name)] for w, name in zip(own, names)]

        def both(name, pieces):
            return [q for w in pieces for q in (w, pair_swap(w, name))]

        def add_pieces(acc, m, x_ref, w_refs, piece_keys, table, counts_ref, where_ref):
            for w_ref, key in zip(w_refs, piece_keys):
                first = place.first(where_ref, key)

                def terms(s, w_ref=w_ref, first=first):
                    return mm(x_ref[:, columns(table[0, first + s])], w_ref[s], NT if m == 2 else NN)

                def store(s, value, first=first):
                    acc[table[1, first + s]] += value

                over_live(live_in(counts_ref[m], first, w_ref.shape[0]), terms, store)

        def begin(m, x, pieces, piece_keys):
            def body(where_ref, counts_ref, table, x_ref, *refs):
                zero(refs[-1])
                add_pieces(refs[-1], m, x_ref, refs[:-1], piece_keys, table, counts_ref, where_ref)

            (acc,) = call(
                body, [where, counts, tables[m]], [x, *pieces], [hidden_f32],
                products=sum(p.shape[0] for p in pieces),
            )
            return acc

        def go_on(m, acc, x, pieces, piece_keys):
            if not pieces:
                return acc

            def body(where_ref, counts_ref, table, acc_in, x_ref, *refs):
                add_pieces(refs[-1], m, x_ref, refs[:-1], piece_keys, table, counts_ref, where_ref)

            (acc,) = call(
                body, [where, counts, tables[m]], [acc, x, *pieces], [hidden_f32],
                products=sum(p.shape[0] for p in pieces), aliases={3: 0},
            )
            return acc

        def relayed(name, pieces, *others):
            out = []
            for w in pieces if halves else []:
                out.append(part_swap(after(w, *others), name))
                others = out[-1:]
            return out

        acc_g = begin(0, tokens, near[0], near_keys)
        acc_u = begin(1, tokens, near[1], near_keys)
        tokens_pair = pair_swap(tokens, "tokens")
        cotangent_pair = pair_swap(cotangent, "cotangent")

        x_g = shift_all("gate", cut[0])
        x_g = after(x_g, acc_g, cotangent_pair)
        x_u = shift_all("up", cut[1], *x_g)
        y_g = relayed("gate", x_g)

        acc_h = begin(2, cotangent, near[2], near_keys)
        direct = [both("gate_x", after(x_g, acc_u))]
        x_u, y_g = after((x_u, y_g), acc_u, acc_h)
        x_d = shift_all("down", cut[2], *x_u)

        low = cut[1].shape[0] // 2
        sizes = (low, cut[1].shape[0] - low)
        n_fresh, n_direct = len(x_u), len(direct_keys)

        def direct_body(where_ref, counts_ref, tg, acc_in, x_ref, *refs):
            w_refs, refs = refs[:n_direct], refs[n_direct:]
            fresh, acc, outs = refs[:n_fresh], refs[n_fresh], refs[n_fresh + 1 :]
            for i, w_ref in enumerate(fresh):
                outs[2 * i][...] = w_ref[:low]
                outs[2 * i + 1][...] = w_ref[low:]
            add_pieces(acc, 0, x_ref, w_refs, direct_keys, tg, counts_ref, where_ref)

        acc_g, *split = call(
            direct_body,
            [where, counts, tables[0]],
            [acc_g, tokens, *direct[0], *x_u],
            [hidden_f32] + [jax.ShapeDtypeStruct((n, size, size), BF16) for n in sizes] * n_fresh,
            products=2 * shard,
            aliases={3: 0},
        )

        def split_swap(name, pieces, halved, half):
            blocks, its_keys = [], []
            for k, w in enumerate(pieces):
                blocks += [w] + [pair_swap(h, name) for h in halved[2 * k : 2 * k + 2]]
                its_keys += [(k + 1, other, half, o) for other, o in ((False, 0), (True, 0), (True, low))]
            return blocks, its_keys

        up_direct, up_keys = split_swap("up_x", x_u, split, near_half)
        all_keys[1] = near_keys + up_keys + relay_keys
        y_u = relayed("up", x_u)
        direct.append(up_direct)
        acc_u = go_on(1, acc_u, tokens, up_direct, up_keys)

        x_d = after(x_d, acc_u)
        y_u = after(y_u, *x_d)
        y_d = relayed("down", x_d, *y_u)
        direct.append(both("down_x", x_d))
        relay = [both("gate_y", after(y_g, *x_d)), both("up_y", y_u)]

        def gate_body(where_ref, counts_ref, tg, acc_in, x_ref, *refs):
            w_refs, silu_ref, slope_ref, acc = refs[:-3], *refs[-3:]
            acc[...] = acc_in[...]
            add_pieces(acc, 0, x_ref, w_refs, relay_keys, tg, counts_ref, where_ref)

            def finish(b, _):
                gate = acc[b]
                sigma = jax.nn.sigmoid(gate)
                silu_ref[b] = gate * sigma
                slope_ref[b] = sigma * (1.0 + gate * (1.0 - sigma))
                return 0

            lax.fori_loop(0, hidden_blocks, finish, 0)

        silu, slope = call(
            gate_body,
            [where, counts, tables[0]],
            [acc_g, tokens, *relay[0]],
            [hidden_f32, hidden_f32],
            scratch=[pltpu.VMEM(hidden_f32.shape, F32)],
            products=shard,
        )
        quarter = token_count // 4

        def up_body(where_ref, counts_ref, tu, acc_in, silu_ref, x_ref, *refs):
            w_refs, acc, h_refs = refs[:-5], refs[-5], refs[-4:]
            add_pieces(acc, 1, x_ref, w_refs, relay_keys, tu, counts_ref, where_ref)

            def finish(b, _):
                hidden = (silu_ref[b] * acc[b]).astype(BF16)
                for i, h_ref in enumerate(h_refs):
                    h_ref[b] = hidden[i * quarter : (i + 1) * quarter]
                return 0

            lax.fori_loop(0, hidden_blocks, finish, 0)

        up_value, *hidden = call(
            up_body,
            [where, counts, tables[1]],
            [acc_u, silu, tokens, *relay[1]],
            [
                hidden_f32,
                *[jax.ShapeDtypeStruct((hidden_blocks, quarter, size), BF16)] * 4,
            ],
            aliases={3: 0},
            products=shard + 20,
        )
        hidden_pair = [pair_swap(h, "hidden") for h in hidden]

        def block_grads(m, ahead, left, right, cuts=(0, shard)):
            spans = [(k, low, high) for k in ahead for low, high in zip(cuts, cuts[1:])]

            n_left, n_both = len(left), len(left) + len(right)

            def body(where_ref, counts_ref, table, *refs):
                ls, rs, outs = refs[:n_left], refs[n_left:n_both], refs[n_both:]
                for (k, low, high), o_ref in zip(spans, outs):
                    first = place.first(where_ref, ((chips - k) % chips, False, None, 0)) + low
                    live = live_in(counts_ref[m], first, high - low)

                    def terms(s, first=first):
                        f, h = table[0, first + s], table[1, first + s]
                        wide, deep = (rs, ls) if m == 2 else (ls, rs)
                        model = jnp.concatenate([ref[:, columns(f)] for ref in wide], axis=0)
                        inner = jnp.concatenate([ref[h] for ref in deep], axis=0)
                        return mm(inner, model, TN) if m == 2 else mm(model, inner, TN)

                    def store(s, value, o_ref=o_ref):
                        o_ref[s] = value.astype(BF16)

                    over_live(live, terms, store)

                    def clear(s, _, o_ref=o_ref):
                        o_ref[s] = jnp.zeros((size, size), BF16)
                        return 0

                    lax.fori_loop(live, high - low, clear, 0)

            return call(
                body,
                [where, counts, tables[m]],
                [*left, *right],
                [jax.ShapeDtypeStruct((high - low, size, size), BF16) for _, low, high in spans],
                products=len(ahead) * shard,
            )

        def total(kept, arrived):
            value = kept.astype(F32)
            for g in arrived:
                value = value + g.astype(F32)
            return value.astype(BF16)[None]

        down_operands = ([*hidden, *hidden_pair], [cotangent, cotangent_pair])
        down_away = block_grads(2, away, *down_operands)
        down_far = [chip_shift(g, k, "down_grad") for g, k in zip(down_away, away)]

        relay.append(both("down_y", after(y_d, *down_away)))
        acc_h = go_on(2, after(acc_h, *down_away), cotangent, direct[2], direct_keys)

        half_tokens = token_count // 2

        def back_body(where_ref, counts_ref, td, acc_in, c_ref, silu_ref, slope_ref, up_ref, *refs):
            outs, acc = refs[-4:-1], refs[-1]
            acc[...] = acc_in[...]
            add_pieces(acc, 2, c_ref, refs[:-4], relay_keys, td, counts_ref, where_ref)

            def finish(b, _):
                grad = acc[b]
                gate = (grad * up_ref[b] * slope_ref[b]).astype(BF16)
                up = (grad * silu_ref[b]).astype(BF16)
                for i in range(2):
                    rows = slice(i * half_tokens, (i + 1) * half_tokens)
                    outs[i][b] = gate[rows]
                outs[2][b] = up
                return 0

            lax.fori_loop(0, hidden_blocks, finish, 0)

        grads = call(
            back_body,
            [where, counts, tables[2]],
            [acc_h, cotangent, silu, slope, up_value, *relay[2]],
            [jax.ShapeDtypeStruct((hidden_blocks, half_tokens, size), BF16)] * 2 + [hidden_bf16],
            scratch=[pltpu.VMEM(hidden_f32.shape, F32)],
            products=shard + 10,
        )
        pieces = [near[m] + direct[m] + relay[m] for m in range(3)]

        width = model_blocks // groups
        chunk = jax.ShapeDtypeStruct((groups // 2, token_count, width * size), BF16)

        def deal(where_ref, acc, outs):
            for i in range(groups):
                to = lax.bitwise_xor(where_ref[3], i) * width
                for j in range(width):
                    outs[i % 2][i // 2, :, j * size : (j + 1) * size] = acc[to + j].astype(BF16)

        def out_body(where_ref, counts_ref, td, *refs):
            h_refs, refs = refs[:4], refs[4:]
            w_refs, outs, acc = refs[: len(every)], refs[len(every) : -1], refs[-1]
            zero(acc)
            for w_ref, key in zip(w_refs, every):
                first = place.first(where_ref, key)

                def terms(s, w_ref=w_ref, first=first):
                    h = td[1, first + s]
                    return mm(jnp.concatenate([h_ref[h] for h_ref in h_refs], axis=0), w_ref[s])

                def store(s, value, first=first):
                    acc[td[0, first + s]] += value

                over_live(live_in(counts_ref[2], first, w_ref.shape[0]), terms, store)
            deal(where_ref, acc, outs)

        model_acc = pltpu.VMEM((model_blocks, token_count, size), F32)
        out_parts = call(
            out_body,
            [where, counts, tables[2]],
            [*after(hidden, *grads), *pieces[2]],
            [chunk] * 2,
            scratch=[model_acc],
            products=4 * shard,
        )

        grads_pair = [pair_swap(g, "grads") for g in grads]
        grads_pair[:2] = after(grads_pair[:2], *out_parts)
        gate_operands = ([tokens, tokens_pair], [*grads[:2], *grads_pair[:2]])
        up_operands = ([tokens, tokens_pair], [grads[2], grads_pair[2]])
        gate_away = block_grads(0, away, *gate_operands)
        up_away = block_grads(1, away, *up_operands)
        down_far = after(down_far, *gate_away)

        def token_body(m, last, where_ref, counts_ref, table, *refs):
            n, n_y = len(all_keys[m]), 1 if m else 2
            ys, w_refs, acc = refs[:n_y], refs[n_y : n_y + n], refs[-1]
            if not last:
                zero(acc)
            for w_ref, key in zip(w_refs, all_keys[m]):
                first = place.first(where_ref, key)

                def terms(s, w_ref=w_ref, first=first):
                    h = table[1, first + s]
                    y = jnp.concatenate([y_ref[h] for y_ref in ys], axis=0)
                    return mm(y, w_ref[s], NT)

                def store(s, value, first=first):
                    acc[table[0, first + s]] += value

                over_live(live_in(counts_ref[m], first, w_ref.shape[0]), terms, store)
            if last:
                deal(where_ref, acc, refs[-3:-1])

        model_f32 = jax.ShapeDtypeStruct((model_blocks, token_count, size), F32)
        (token_acc,) = call(
            functools.partial(token_body, 0, False),
            [where, counts, tables[0]],
            [*after(grads[:2], *gate_away), *pieces[0]],
            [model_f32],
            products=4 * shard,
        )
        down_far = after(down_far, token_acc)
        y_up = after(grads[2], *down_far)
        *token_parts, _ = call(
            functools.partial(token_body, 1, True),
            [where, counts, tables[1]],
            [y_up, *pieces[1], token_acc],
            [chunk] * 2 + [model_f32],
            products=4 * shard,
            aliases={4 + len(pieces[1]): 2},
        )

        def swap_groups(name, chunks, *others):
            kept, sent = chunks
            bit, first = 1, None
            while True:
                arrived = group_swap(sent, bit, name)
                first = arrived if first is None else first
                bit *= 2
                if bit == groups:
                    return first, kept, arrived
                value = (kept.astype(F32) + after(arrived, *others).astype(F32)).astype(BF16)
                kept, sent = value[0::2], value[1::2]

        def last_sum(kept, arrived, *others):
            value = kept.astype(F32) + after(arrived, *others).astype(F32)
            return value[0].astype(BF16)

        gate_sent = after(gate_away, *down_far)
        gate_far = [chip_shift(g, k, "gate_grad") for g, k in zip(gate_sent, away)]
        out_first, *out_terms = swap_groups("out", out_parts, *token_parts)
        up_sent = after(up_away, out_first)
        up_far = [chip_shift(g, k, "up_grad") for g, k in zip(up_sent, away)]
        late_h, late_t = after(hidden, out_first), after(tokens, *gate_far)
        (down_kept,) = block_grads(2, (0,), [*late_h, *hidden_pair], down_operands[1])
        (gate_kept,) = block_grads(0, (0,), [late_t, tokens_pair], gate_operands[1])
        (up_kept,) = block_grads(1, (0,), [late_t, tokens_pair], up_operands[1])
        down_grad = total(down_kept, down_far)
        gate_far = after(gate_far, down_grad)
        layer_out = last_sum(*out_terms, *gate_far)
        _, *token_terms = swap_groups("token", token_parts, *gate_far)
        gate_grad = total(gate_kept, gate_far)
        token_grad = last_sum(*token_terms, layer_out, gate_grad)
        up_grad = total(up_kept, after(up_far, token_grad))
        return layer_out, token_grad, gate_grad, up_grad, down_grad

    return per_device


def solution(mesh):
    return jax.shard_map(
        make(mesh),
        mesh=mesh,
        in_specs=(
            P(("parts", "dp"), None),
            P(("parts", "dp"), None),
            P("tensor", "dp", None, None),
            P("tensor", "dp", None, None),
            P("tensor", "dp", None, None),
            P(None, "tensor", None),
            P(None, "tensor", None),
            P(None, "tensor", None),
            P(None, "tensor"),
        ),
        out_specs=(
            P(("parts", "dp"), "tensor"),
            P(("parts", "dp"), "tensor"),
            P(("parts", "tensor"), "dp", None, None),
            P(("parts", "tensor"), "dp", None, None),
            P(("parts", "tensor"), "dp", None, None),
        ),
        check_vma=False,
    )
```

```python
import functools

import jax
import jax.numpy as jnp
from jax import lax
from jax.experimental import pallas as pl
from jax.experimental.pallas import tpu as pltpu
from jax.sharding import PartitionSpec as P

FF = 14336
F32 = jnp.float32
BF16 = jnp.bfloat16
UNROLL = 7
NN = (((1,), (0,)), ((), ()))
NT = (((1,), (1,)), ((), ()))
TN = (((0,), (0,)), ((), ()))

VMEM = pl.BlockSpec(memory_space=pltpu.VMEM)
SMEM = pl.BlockSpec(memory_space=pltpu.SMEM)


def mm(left, right, dims=NN):
    return lax.dot_general(left, right, dims, preferred_element_type=F32)


def call(body, ints, arrays, outs, scratch=(), products=0, aliases=None):
    size = lambda a: a.size * a.dtype.itemsize
    total = sum(size(a) for a in arrays) + sum(size(o) for o in outs)
    held = total + sum(s.inner_aval.size * s.inner_aval.dtype.itemsize if hasattr(s, "inner_aval") else 0 for s in scratch)
    return pl.pallas_call(
        body,
        out_shape=outs,
        in_specs=[SMEM] * len(ints) + [VMEM] * len(arrays),
        out_specs=[VMEM] * len(outs),
        scratch_shapes=list(scratch),
        input_output_aliases=aliases or {},
        compiler_params=pltpu.CompilerParams(vmem_limit_bytes=held + (12 << 20)),
        cost_estimate=pl.CostEstimate(
            flops=products, bytes_accessed=products, transcendentals=0
        ),
    )(*ints, *arrays)


class Place:
    def __init__(self, chips, parts, groups, shard):
        self.chips, self.parts, self.groups, self.shard = chips, parts, groups, shard

    def first(self, where, piece):
        chip, core, part = where[0], where[1], where[2]
        back, other, half, offset = piece
        chip = lax.rem(chip + (self.chips - back), self.chips)
        core = 1 - core if other else core
        start = (chip * 2 + core) * self.shard
        if half is not None:
            start = start + (1 - part if half else part) * (self.shard // 2)
        return start + offset


def over_live(live, terms, store):
    def several(step, _):
        slots = [step * UNROLL + u for u in range(UNROLL)]
        values = [terms(slot) for slot in slots]
        for slot, value in zip(slots, values):
            store(slot, value)
        return 0

    rounds = lax.div(live, UNROLL)
    lax.fori_loop(0, rounds, several, 0)
    done = rounds * UNROLL

    @pl.when(done < live)
    def _():
        slots = [jnp.minimum(done + u, live - 1) for u in range(UNROLL - 1)]
        values = [terms(slot) for slot in slots]
        store(slots[0], values[0])
        for u in range(1, UNROLL - 1):

            @pl.when(done + u < live)
            def _(u=u):
                store(slots[u], values[u])


def live_in(count, first, extent):
    return jnp.clip(count - first, 0, extent)


def columns(block, size=128):
    return pl.ds(pl.multiple_of(block * size, size), size)


def after(value, *others):
    return lax.optimization_barrier((value, others))[0]


def zero(acc):
    acc[...] = jnp.zeros(acc.shape, acc.dtype)


def make(mesh):
    parts = mesh.shape["parts"]
    dp = mesh.shape["dp"]
    groups = mesh.shape["tensor"]
    chips = dp // 2

    def pair_swap(a, name):
        with jax.named_scope(name + "_core"):
            return lax.ppermute(a, "dp", [(i, i ^ 1) for i in range(dp)])

    def chip_shift(a, k, name):
        with jax.named_scope(name + "_chip"):
            return lax.ppermute(
                a, "dp", [(i, ((i // 2 + k) % chips) * 2 + i % 2) for i in range(dp)]
            )

    def part_swap(a, name):
        with jax.named_scope(name + "_part"):
            return lax.ppermute(a, "parts", [(0, 1), (1, 0)])

    def group_swap(a, bit, name):
        with jax.named_scope(name + "_group"):
            return lax.ppermute(a, "tensor", [(i, i ^ bit) for i in range(groups)])

    def per_device(
        tokens, cotangent, gate_blocks, up_blocks, down_blocks, gate_index, up_index, down_index, block_counts
    ):
        token_count, model_width = tokens.shape
        size = gate_blocks.shape[2]
        shard = gate_blocks.shape[1]
        model_blocks = model_width // size
        hidden_blocks = FF // size // groups
        halves = parts == 2 and shard % 2 == 0
        place = Place(chips, parts, groups, shard)
        at = lax.axis_index("dp")
        part = lax.axis_index("parts")
        where = jnp.stack([at // 2, at % 2, part, lax.axis_index("tensor")]).astype(jnp.int32)
        tables = [gate_index[:, 0], up_index[:, 0], down_index[:, 0]]
        counts = block_counts[:, 0]

        hidden_f32 = jax.ShapeDtypeStruct((hidden_blocks, token_count, size), F32)
        hidden_bf16 = jax.ShapeDtypeStruct((hidden_blocks, token_count, size), BF16)

        own = [gate_blocks[0], up_blocks[0], down_blocks[0]]
        near_keys = [(0, False, None, 0), (0, True, None, 0)]
        away = tuple(range(1, chips))
        near_half, far_half = (False, True) if halves else (None, None)
        direct_keys = [(k, other, near_half, 0) for k in away for other in (False, True)]
        relay_keys = [(k, other, far_half, 0) for k in away for other in (False, True)] if halves else []
        every = near_keys + direct_keys + relay_keys
        all_keys = [every, every, every]
        cut = own
        if halves:
            cut = [
                lax.dynamic_slice_in_dim(w, part * (shard // 2), shard // 2, 0) for w in own
            ]

        def shift_all(name, blocks, *others):
            arrived = []
            for k in away:
                arrived.append(chip_shift(after(blocks, *others), k, name))
                others = arrived[-1:]
            return arrived

        names = ("gate", "up", "down")
        near = [[w, pair_swap(w, name)] for w, name in zip(own, names)]

        def both(name, pieces):
            return [q for w in pieces for q in (w, pair_swap(w, name))]

        def add_pieces(acc, m, x_ref, w_refs, piece_keys, table, counts_ref, where_ref):
            for w_ref, key in zip(w_refs, piece_keys):
                first = place.first(where_ref, key)

                def terms(s, w_ref=w_ref, first=first):
                    return mm(x_ref[:, columns(table[0, first + s])], w_ref[s], NT if m == 2 else NN)

                def store(s, value, first=first):
                    acc[table[1, first + s]] += value

                over_live(live_in(counts_ref[m], first, w_ref.shape[0]), terms, store)

        def begin(m, x, pieces, piece_keys):
            def body(where_ref, counts_ref, table, x_ref, *refs):
                zero(refs[-1])
                add_pieces(refs[-1], m, x_ref, refs[:-1], piece_keys, table, counts_ref, where_ref)

            (acc,) = call(
                body, [where, counts, tables[m]], [x, *pieces], [hidden_f32],
                products=sum(p.shape[0] for p in pieces),
            )
            return acc

        def go_on(m, acc, x, pieces, piece_keys):
            if not pieces:
                return acc

            def body(where_ref, counts_ref, table, acc_in, x_ref, *refs):
                add_pieces(refs[-1], m, x_ref, refs[:-1], piece_keys, table, counts_ref, where_ref)

            (acc,) = call(
                body, [where, counts, tables[m]], [acc, x, *pieces], [hidden_f32],
                products=sum(p.shape[0] for p in pieces), aliases={3: 0},
            )
            return acc

        def relayed(name, pieces, *others):
            out = []
            for w in pieces if halves else []:
                out.append(part_swap(after(w, *others), name))
                others = out[-1:]
            return out

        acc_g = begin(0, tokens, near[0], near_keys)
        acc_u = begin(1, tokens, near[1], near_keys)
        tokens_pair = pair_swap(tokens, "tokens")
        cotangent_pair = pair_swap(cotangent, "cotangent")

        x_g = shift_all("gate", cut[0])
        x_g = after(x_g, acc_g, cotangent_pair)
        x_u = shift_all("up", cut[1], *x_g)
        y_g = relayed("gate", x_g)

        acc_h = begin(2, cotangent, near[2], near_keys)
        direct = [both("gate_x", after(x_g, acc_u))]
        x_u, y_g = after((x_u, y_g), acc_u, acc_h)
        x_d = shift_all("down", cut[2], *x_u)

        low = cut[1].shape[0] // 2
        sizes = (low, cut[1].shape[0] - low)
        n_fresh, n_direct = len(x_u), len(direct_keys)

        def direct_body(where_ref, counts_ref, tg, acc_in, x_ref, *refs):
            w_refs, refs = refs[:n_direct], refs[n_direct:]
            fresh, acc, outs = refs[:n_fresh], refs[n_fresh], refs[n_fresh + 1 :]
            for i, w_ref in enumerate(fresh):
                outs[2 * i][...] = w_ref[:low]
                outs[2 * i + 1][...] = w_ref[low:]
            add_pieces(acc, 0, x_ref, w_refs, direct_keys, tg, counts_ref, where_ref)

        acc_g, *split = call(
            direct_body,
            [where, counts, tables[0]],
            [acc_g, tokens, *direct[0], *x_u],
            [hidden_f32] + [jax.ShapeDtypeStruct((n, size, size), BF16) for n in sizes] * n_fresh,
            products=2 * shard,
            aliases={3: 0},
        )

        def split_swap(name, pieces, halved, half):
            blocks, its_keys = [], []
            for k, w in enumerate(pieces):
                blocks += [w] + [pair_swap(h, name) for h in halved[2 * k : 2 * k + 2]]
                its_keys += [(k + 1, other, half, o) for other, o in ((False, 0), (True, 0), (True, low))]
            return blocks, its_keys

        up_direct, up_keys = split_swap("up_x", x_u, split, near_half)
        all_keys[1] = near_keys + up_keys + relay_keys
        y_u = relayed("up", x_u)
        direct.append(up_direct)
        acc_u = go_on(1, acc_u, tokens, up_direct, up_keys)

        x_d = after(x_d, acc_u)
        y_u = after(y_u, *x_d)
        y_d = relayed("down", x_d, *y_u)
        direct.append(both("down_x", x_d))
        relay = [both("gate_y", after(y_g, *x_d)), both("up_y", y_u)]

        def gate_body(where_ref, counts_ref, tg, acc_in, x_ref, *refs):
            w_refs, silu_ref, slope_ref, acc = refs[:-3], *refs[-3:]
            acc[...] = acc_in[...]
            add_pieces(acc, 0, x_ref, w_refs, relay_keys, tg, counts_ref, where_ref)

            def finish(b, _):
                gate = acc[b]
                sigma = jax.nn.sigmoid(gate)
                silu_ref[b] = gate * sigma
                slope_ref[b] = sigma * (1.0 + gate * (1.0 - sigma))
                return 0

            lax.fori_loop(0, hidden_blocks, finish, 0)

        silu, slope = call(
            gate_body,
            [where, counts, tables[0]],
            [acc_g, tokens, *relay[0]],
            [hidden_f32, hidden_f32],
            scratch=[pltpu.VMEM(hidden_f32.shape, F32)],
            products=shard,
        )
        quarter = token_count // 4

        def up_body(where_ref, counts_ref, tu, acc_in, silu_ref, x_ref, *refs):
            w_refs, acc, h_refs = refs[:-5], refs[-5], refs[-4:]
            add_pieces(acc, 1, x_ref, w_refs, relay_keys, tu, counts_ref, where_ref)

            def finish(b, _):
                hidden = (silu_ref[b] * acc[b]).astype(BF16)
                for i, h_ref in enumerate(h_refs):
                    h_ref[b] = hidden[i * quarter : (i + 1) * quarter]
                return 0

            lax.fori_loop(0, hidden_blocks, finish, 0)

        up_value, *hidden = call(
            up_body,
            [where, counts, tables[1]],
            [acc_u, silu, tokens, *relay[1]],
            [
                hidden_f32,
                *[jax.ShapeDtypeStruct((hidden_blocks, quarter, size), BF16)] * 4,
            ],
            aliases={3: 0},
            products=shard + 20,
        )
        hidden_pair = [pair_swap(h, "hidden") for h in hidden]

        def block_grads(m, ahead, left, right, cuts=(0, shard)):
            spans = [(k, low, high) for k in ahead for low, high in zip(cuts, cuts[1:])]

            n_left, n_both = len(left), len(left) + len(right)

            def body(where_ref, counts_ref, table, *refs):
                ls, rs, outs = refs[:n_left], refs[n_left:n_both], refs[n_both:]
                for (k, low, high), o_ref in zip(spans, outs):
                    first = place.first(where_ref, ((chips - k) % chips, False, None, 0)) + low
                    live = live_in(counts_ref[m], first, high - low)

                    def terms(s, first=first):
                        f, h = table[0, first + s], table[1, first + s]
                        wide, deep = (rs, ls) if m == 2 else (ls, rs)
                        model = jnp.concatenate([ref[:, columns(f)] for ref in wide], axis=0)
                        inner = jnp.concatenate([ref[h] for ref in deep], axis=0)
                        return mm(inner, model, TN) if m == 2 else mm(model, inner, TN)

                    def store(s, value, o_ref=o_ref):
                        o_ref[s] = value.astype(BF16)

                    over_live(live, terms, store)

                    def clear(s, _, o_ref=o_ref):
                        o_ref[s] = jnp.zeros((size, size), BF16)
                        return 0

                    lax.fori_loop(live, high - low, clear, 0)

            return call(
                body,
                [where, counts, tables[m]],
                [*left, *right],
                [jax.ShapeDtypeStruct((high - low, size, size), BF16) for _, low, high in spans],
                products=len(ahead) * shard,
            )

        def total(kept, arrived):
            value = kept.astype(F32)
            for g in arrived:
                value = value + g.astype(F32)
            return value.astype(BF16)[None]

        down_operands = ([*hidden, *hidden_pair], [cotangent, cotangent_pair])
        down_away = block_grads(2, away, *down_operands)
        down_far = [chip_shift(g, k, "down_grad") for g, k in zip(down_away, away)]

        relay.append(both("down_y", after(y_d, *down_away)))
        acc_h = go_on(2, after(acc_h, *down_away), cotangent, direct[2], direct_keys)

        half_tokens = token_count // 2

        def back_body(where_ref, counts_ref, td, acc_in, c_ref, silu_ref, slope_ref, up_ref, *refs):
            outs, acc = refs[-4:-1], refs[-1]
            acc[...] = acc_in[...]
            add_pieces(acc, 2, c_ref, refs[:-4], relay_keys, td, counts_ref, where_ref)

            def finish(b, _):
                grad = acc[b]
                gate = (grad * up_ref[b] * slope_ref[b]).astype(BF16)
                up = (grad * silu_ref[b]).astype(BF16)
                for i in range(2):
                    rows = slice(i * half_tokens, (i + 1) * half_tokens)
                    outs[i][b] = gate[rows]
                outs[2][b] = up
                return 0

            lax.fori_loop(0, hidden_blocks, finish, 0)

        grads = call(
            back_body,
            [where, counts, tables[2]],
            [acc_h, cotangent, silu, slope, up_value, *relay[2]],
            [jax.ShapeDtypeStruct((hidden_blocks, half_tokens, size), BF16)] * 2 + [hidden_bf16],
            scratch=[pltpu.VMEM(hidden_f32.shape, F32)],
            products=shard + 10,
        )
        pieces = [near[m] + direct[m] + relay[m] for m in range(3)]

        width = model_blocks // groups
        chunk = jax.ShapeDtypeStruct((groups // 2, token_count, width * size), BF16)

        def deal(where_ref, acc, outs):
            for i in range(groups):
                to = lax.bitwise_xor(where_ref[3], i) * width
                for j in range(width):
                    outs[i % 2][i // 2, :, j * size : (j + 1) * size] = acc[to + j].astype(BF16)

        def out_body(where_ref, counts_ref, td, *refs):
            h_refs, refs = refs[:4], refs[4:]
            w_refs, outs, acc = refs[: len(every)], refs[len(every) : -1], refs[-1]
            zero(acc)
            for w_ref, key in zip(w_refs, every):
                first = place.first(where_ref, key)

                def terms(s, w_ref=w_ref, first=first):
                    h = td[1, first + s]
                    return mm(jnp.concatenate([h_ref[h] for h_ref in h_refs], axis=0), w_ref[s])

                def store(s, value, first=first):
                    acc[td[0, first + s]] += value

                over_live(live_in(counts_ref[2], first, w_ref.shape[0]), terms, store)
            deal(where_ref, acc, outs)

        model_acc = pltpu.VMEM((model_blocks, token_count, size), F32)
        out_parts = call(
            out_body,
            [where, counts, tables[2]],
            [*after(hidden, *grads), *pieces[2]],
            [chunk] * 2,
            scratch=[model_acc],
            products=4 * shard,
        )

        grads_pair = [pair_swap(g, "grads") for g in grads]
        grads_pair[:2] = after(grads_pair[:2], *out_parts)
        gate_operands = ([tokens, tokens_pair], [*grads[:2], *grads_pair[:2]])
        up_operands = ([tokens, tokens_pair], [grads[2], grads_pair[2]])
        gate_away = block_grads(0, away, *gate_operands)
        up_away = block_grads(1, away, *up_operands)
        down_far = after(down_far, *gate_away)

        def token_body(m, last, where_ref, counts_ref, table, *refs):
            n, n_y = len(all_keys[m]), 1 if m else 2
            ys, w_refs, acc = refs[:n_y], refs[n_y : n_y + n], refs[-1]
            if not last:
                zero(acc)
            for w_ref, key in zip(w_refs, all_keys[m]):
                first = place.first(where_ref, key)

                def terms(s, w_ref=w_ref, first=first):
                    h = table[1, first + s]
                    y = jnp.concatenate([y_ref[h] for y_ref in ys], axis=0)
                    return mm(y, w_ref[s], NT)

                def store(s, value, first=first):
                    acc[table[0, first + s]] += value

                over_live(live_in(counts_ref[m], first, w_ref.shape[0]), terms, store)
            if last:
                deal(where_ref, acc, refs[-3:-1])

        model_f32 = jax.ShapeDtypeStruct((model_blocks, token_count, size), F32)
        (token_acc,) = call(
            functools.partial(token_body, 0, False),
            [where, counts, tables[0]],
            [*after(grads[:2], *gate_away), *pieces[0]],
            [model_f32],
            products=4 * shard,
        )
        down_far = after(down_far, token_acc)
        y_up = after(grads[2], *down_far)
        *token_parts, _ = call(
            functools.partial(token_body, 1, True),
            [where, counts, tables[1]],
            [y_up, *pieces[1], token_acc],
            [chunk] * 2 + [model_f32],
            products=4 * shard,
            aliases={4 + len(pieces[1]): 2},
        )

        def swap_groups(name, chunks, *others):
            kept, sent = chunks
            bit, first = 1, None
            while True:
                arrived = group_swap(sent, bit, name)
                first = arrived if first is None else first
                bit *= 2
                if bit == groups:
                    return first, kept, arrived
                value = (kept.astype(F32) + after(arrived, *others).astype(F32)).astype(BF16)
                kept, sent = value[0::2], value[1::2]

        def last_sum(kept, arrived, *others):
            value = kept.astype(F32) + after(arrived, *others).astype(F32)
            return value[0].astype(BF16)

        gate_sent = after(gate_away, *down_far)
        gate_far = [chip_shift(g, k, "gate_grad") for g, k in zip(gate_sent, away)]
        out_first, *out_terms = swap_groups("out", after(out_parts, *gate_away), *token_parts)
        up_sent = after(up_away, out_first)
        up_far = [chip_shift(g, k, "up_grad") for g, k in zip(up_sent, away)]
        late_h, late_t = after(hidden, out_first), after(tokens, *gate_far)
        (down_kept,) = block_grads(2, (0,), [*late_h, *hidden_pair], down_operands[1])
        (gate_kept,) = block_grads(0, (0,), [late_t, tokens_pair], gate_operands[1])
        (up_kept,) = block_grads(1, (0,), [late_t, tokens_pair], up_operands[1])
        down_grad = total(down_kept, down_far)
        gate_far = after(gate_far, down_grad)
        layer_out = last_sum(*out_terms, *gate_far)
        _, *token_terms = swap_groups("token", token_parts, *gate_far)
        gate_grad = total(gate_kept, gate_far)
        token_grad = last_sum(*token_terms, layer_out, gate_grad)
        up_grad = total(up_kept, after(up_far, token_grad))
        return layer_out, token_grad, gate_grad, up_grad, down_grad

    return per_device


def solution(mesh):
    return jax.shard_map(
        make(mesh),
        mesh=mesh,
        in_specs=(
            P(("parts", "dp"), None),
            P(("parts", "dp"), None),
            P("tensor", "dp", None, None),
            P("tensor", "dp", None, None),
            P("tensor", "dp", None, None),
            P(None, "tensor", None),
            P(None, "tensor", None),
            P(None, "tensor", None),
            P(None, "tensor"),
        ),
        out_specs=(
            P(("parts", "dp"), "tensor"),
            P(("parts", "dp"), "tensor"),
            P(("parts", "tensor"), "dp", None, None),
            P(("parts", "tensor"), "dp", None, None),
            P(("parts", "tensor"), "dp", None, None),
        ),
        check_vma=False,
    )
```

```python
import functools

import jax
import jax.numpy as jnp
from jax import lax
from jax.experimental import pallas as pl
from jax.experimental.pallas import tpu as pltpu
from jax.sharding import PartitionSpec as P

FF = 14336
F32 = jnp.float32
BF16 = jnp.bfloat16
UNROLL = 7
NN = (((1,), (0,)), ((), ()))
NT = (((1,), (1,)), ((), ()))
TN = (((0,), (0,)), ((), ()))

VMEM = pl.BlockSpec(memory_space=pltpu.VMEM)
SMEM = pl.BlockSpec(memory_space=pltpu.SMEM)


def mm(left, right, dims=NN):
    return lax.dot_general(left, right, dims, preferred_element_type=F32)


def call(body, ints, arrays, outs, scratch=(), products=0, aliases=None):
    size = lambda a: a.size * a.dtype.itemsize
    total = sum(size(a) for a in arrays) + sum(size(o) for o in outs)
    held = total + sum(s.inner_aval.size * s.inner_aval.dtype.itemsize if hasattr(s, "inner_aval") else 0 for s in scratch)
    return pl.pallas_call(
        body,
        out_shape=outs,
        in_specs=[SMEM] * len(ints) + [VMEM] * len(arrays),
        out_specs=[VMEM] * len(outs),
        scratch_shapes=list(scratch),
        input_output_aliases=aliases or {},
        compiler_params=pltpu.CompilerParams(vmem_limit_bytes=held + (12 << 20)),
        cost_estimate=pl.CostEstimate(
            flops=products, bytes_accessed=products, transcendentals=0
        ),
    )(*ints, *arrays)


class Place:
    def __init__(self, chips, parts, groups, shard):
        self.chips, self.parts, self.groups, self.shard = chips, parts, groups, shard

    def first(self, where, piece):
        chip, core, part = where[0], where[1], where[2]
        back, other, half, offset = piece
        chip = lax.rem(chip + (self.chips - back), self.chips)
        core = 1 - core if other else core
        start = (chip * 2 + core) * self.shard
        if half is not None:
            start = start + (1 - part if half else part) * (self.shard // 2)
        return start + offset


def over_live(live, terms, store):
    def several(step, _):
        slots = [step * UNROLL + u for u in range(UNROLL)]
        values = [terms(slot) for slot in slots]
        for slot, value in zip(slots, values):
            store(slot, value)
        return 0

    rounds = lax.div(live, UNROLL)
    lax.fori_loop(0, rounds, several, 0)
    done = rounds * UNROLL

    @pl.when(done < live)
    def _():
        slots = [jnp.minimum(done + u, live - 1) for u in range(UNROLL - 1)]
        values = [terms(slot) for slot in slots]
        store(slots[0], values[0])
        for u in range(1, UNROLL - 1):

            @pl.when(done + u < live)
            def _(u=u):
                store(slots[u], values[u])


def live_in(count, first, extent):
    return jnp.clip(count - first, 0, extent)


def columns(block, size=128):
    return pl.ds(pl.multiple_of(block * size, size), size)


def after(value, *others):
    return lax.optimization_barrier((value, others))[0]


def zero(acc):
    acc[...] = jnp.zeros(acc.shape, acc.dtype)


def make(mesh):
    parts = mesh.shape["parts"]
    dp = mesh.shape["dp"]
    groups = mesh.shape["tensor"]
    chips = dp // 2

    def pair_swap(a, name):
        with jax.named_scope(name + "_core"):
            return lax.ppermute(a, "dp", [(i, i ^ 1) for i in range(dp)])

    def chip_shift(a, k, name):
        with jax.named_scope(name + "_chip"):
            return lax.ppermute(
                a, "dp", [(i, ((i // 2 + k) % chips) * 2 + i % 2) for i in range(dp)]
            )

    def part_swap(a, name):
        with jax.named_scope(name + "_part"):
            return lax.ppermute(a, "parts", [(0, 1), (1, 0)])

    def group_swap(a, bit, name):
        with jax.named_scope(name + "_group"):
            return lax.ppermute(a, "tensor", [(i, i ^ bit) for i in range(groups)])

    def per_device(
        tokens, cotangent, gate_blocks, up_blocks, down_blocks, gate_index, up_index, down_index, block_counts
    ):
        token_count, model_width = tokens.shape
        size = gate_blocks.shape[2]
        shard = gate_blocks.shape[1]
        model_blocks = model_width // size
        hidden_blocks = FF // size // groups
        halves = parts == 2 and shard % 2 == 0
        place = Place(chips, parts, groups, shard)
        at = lax.axis_index("dp")
        part = lax.axis_index("parts")
        where = jnp.stack([at // 2, at % 2, part, lax.axis_index("tensor")]).astype(jnp.int32)
        tables = [gate_index[:, 0], up_index[:, 0], down_index[:, 0]]
        counts = block_counts[:, 0]

        hidden_f32 = jax.ShapeDtypeStruct((hidden_blocks, token_count, size), F32)
        hidden_bf16 = jax.ShapeDtypeStruct((hidden_blocks, token_count, size), BF16)

        own = [gate_blocks[0], up_blocks[0], down_blocks[0]]
        near_keys = [(0, False, None, 0), (0, True, None, 0)]
        away = tuple(range(1, chips))
        near_half, far_half = (False, True) if halves else (None, None)
        direct_keys = [(k, other, near_half, 0) for k in away for other in (False, True)]
        relay_keys = [(k, other, far_half, 0) for k in away for other in (False, True)] if halves else []
        every = near_keys + direct_keys + relay_keys
        all_keys = [every, every, every]
        cut = own
        if halves:
            cut = [
                lax.dynamic_slice_in_dim(w, part * (shard // 2), shard // 2, 0) for w in own
            ]

        def shift_all(name, blocks, *others):
            arrived = []
            for k in away:
                arrived.append(chip_shift(after(blocks, *others), k, name))
                others = arrived[-1:]
            return arrived

        names = ("gate", "up", "down")
        near = [[w, pair_swap(w, name)] for w, name in zip(own, names)]

        def both(name, pieces):
            return [q for w in pieces for q in (w, pair_swap(w, name))]

        def add_pieces(acc, m, x_ref, w_refs, piece_keys, table, counts_ref, where_ref):
            for w_ref, key in zip(w_refs, piece_keys):
                first = place.first(where_ref, key)

                def terms(s, w_ref=w_ref, first=first):
                    return mm(x_ref[:, columns(table[0, first + s])], w_ref[s], NT if m == 2 else NN)

                def store(s, value, first=first):
                    acc[table[1, first + s]] += value

                over_live(live_in(counts_ref[m], first, w_ref.shape[0]), terms, store)

        def begin(m, x, pieces, piece_keys):
            def body(where_ref, counts_ref, table, x_ref, *refs):
                zero(refs[-1])
                add_pieces(refs[-1], m, x_ref, refs[:-1], piece_keys, table, counts_ref, where_ref)

            (acc,) = call(
                body, [where, counts, tables[m]], [x, *pieces], [hidden_f32],
                products=sum(p.shape[0] for p in pieces),
            )
            return acc

        def go_on(m, acc, x, pieces, piece_keys):
            if not pieces:
                return acc

            def body(where_ref, counts_ref, table, acc_in, x_ref, *refs):
                add_pieces(refs[-1], m, x_ref, refs[:-1], piece_keys, table, counts_ref, where_ref)

            (acc,) = call(
                body, [where, counts, tables[m]], [acc, x, *pieces], [hidden_f32],
                products=sum(p.shape[0] for p in pieces), aliases={3: 0},
            )
            return acc

        def relayed(name, pieces, *others):
            out = []
            for w in pieces if halves else []:
                out.append(part_swap(after(w, *others), name))
                others = out[-1:]
            return out

        acc_g = begin(0, tokens, near[0], near_keys)
        acc_u = begin(1, tokens, near[1], near_keys)
        tokens_pair = pair_swap(tokens, "tokens")
        cotangent_pair = pair_swap(cotangent, "cotangent")

        x_g = shift_all("gate", cut[0])
        x_g = after(x_g, acc_g, cotangent_pair)
        x_u = shift_all("up", cut[1], *x_g)
        y_g = relayed("gate", x_g)

        acc_h = begin(2, cotangent, near[2], near_keys)
        direct = [both("gate_x", after(x_g, acc_u))]
        x_u, y_g = after((x_u, y_g), acc_u, acc_h)
        x_d = shift_all("down", cut[2], *x_u)

        low = cut[1].shape[0] // 2
        sizes = (low, cut[1].shape[0] - low)
        n_fresh, n_direct = len(x_u), len(direct_keys)

        def direct_body(where_ref, counts_ref, tg, acc_in, x_ref, *refs):
            w_refs, refs = refs[:n_direct], refs[n_direct:]
            fresh, acc, outs = refs[:n_fresh], refs[n_fresh], refs[n_fresh + 1 :]
            for i, w_ref in enumerate(fresh):
                outs[2 * i][...] = w_ref[:low]
                outs[2 * i + 1][...] = w_ref[low:]
            add_pieces(acc, 0, x_ref, w_refs, direct_keys, tg, counts_ref, where_ref)

        acc_g, *split = call(
            direct_body,
            [where, counts, tables[0]],
            [acc_g, tokens, *direct[0], *x_u],
            [hidden_f32] + [jax.ShapeDtypeStruct((n, size, size), BF16) for n in sizes] * n_fresh,
            products=2 * shard,
            aliases={3: 0},
        )

        def split_swap(name, pieces, halved, half):
            blocks, its_keys = [], []
            for k, w in enumerate(pieces):
                blocks += [w] + [pair_swap(h, name) for h in halved[2 * k : 2 * k + 2]]
                its_keys += [(k + 1, other, half, o) for other, o in ((False, 0), (True, 0), (True, low))]
            return blocks, its_keys

        up_direct, up_keys = split_swap("up_x", x_u, split, near_half)
        all_keys[1] = near_keys + up_keys + relay_keys
        y_u = relayed("up", x_u)
        direct.append(up_direct)
        acc_u = go_on(1, acc_u, tokens, up_direct, up_keys)

        x_d = after(x_d, acc_u)
        y_u = after(y_u, *x_d)
        y_d = relayed("down", x_d, *y_u)
        direct.append(both("down_x", x_d))
        relay = [both("gate_y", after(y_g, *x_d)), both("up_y", y_u)]

        def gate_body(where_ref, counts_ref, tg, acc_in, x_ref, *refs):
            w_refs, silu_ref, slope_ref, acc = refs[:-3], *refs[-3:]
            acc[...] = acc_in[...]
            add_pieces(acc, 0, x_ref, w_refs, relay_keys, tg, counts_ref, where_ref)

            def finish(b, _):
                gate = acc[b]
                sigma = jax.nn.sigmoid(gate)
                silu_ref[b] = gate * sigma
                slope_ref[b] = sigma * (1.0 + gate * (1.0 - sigma))
                return 0

            lax.fori_loop(0, hidden_blocks, finish, 0)

        silu, slope = call(
            gate_body,
            [where, counts, tables[0]],
            [acc_g, tokens, *relay[0]],
            [hidden_f32, hidden_f32],
            scratch=[pltpu.VMEM(hidden_f32.shape, F32)],
            products=shard,
        )
        quarter = token_count // 4

        def up_body(where_ref, counts_ref, tu, acc_in, silu_ref, x_ref, *refs):
            w_refs, acc, h_refs = refs[:-5], refs[-5], refs[-4:]
            add_pieces(acc, 1, x_ref, w_refs, relay_keys, tu, counts_ref, where_ref)

            def finish(b, _):
                hidden = (silu_ref[b] * acc[b]).astype(BF16)
                for i, h_ref in enumerate(h_refs):
                    h_ref[b] = hidden[i * quarter : (i + 1) * quarter]
                return 0

            lax.fori_loop(0, hidden_blocks, finish, 0)

        up_value, *hidden = call(
            up_body,
            [where, counts, tables[1]],
            [acc_u, silu, tokens, *relay[1]],
            [
                hidden_f32,
                *[jax.ShapeDtypeStruct((hidden_blocks, quarter, size), BF16)] * 4,
            ],
            aliases={3: 0},
            products=shard + 20,
        )
        hidden_pair = [pair_swap(h, "hidden") for h in hidden]

        def block_grads(m, ahead, left, right, cuts=(0, shard)):
            spans = [(k, low, high) for k in ahead for low, high in zip(cuts, cuts[1:])]

            n_left, n_both = len(left), len(left) + len(right)

            def body(where_ref, counts_ref, table, *refs):
                ls, rs, outs = refs[:n_left], refs[n_left:n_both], refs[n_both:]
                for (k, low, high), o_ref in zip(spans, outs):
                    first = place.first(where_ref, ((chips - k) % chips, False, None, 0)) + low
                    live = live_in(counts_ref[m], first, high - low)

                    def terms(s, first=first):
                        f, h = table[0, first + s], table[1, first + s]
                        wide, deep = (rs, ls) if m == 2 else (ls, rs)
                        model = jnp.concatenate([ref[:, columns(f)] for ref in wide], axis=0)
                        inner = jnp.concatenate([ref[h] for ref in deep], axis=0)
                        return mm(inner, model, TN) if m == 2 else mm(model, inner, TN)

                    def store(s, value, o_ref=o_ref):
                        o_ref[s] = value.astype(BF16)

                    over_live(live, terms, store)

                    def clear(s, _, o_ref=o_ref):
                        o_ref[s] = jnp.zeros((size, size), BF16)
                        return 0

                    lax.fori_loop(live, high - low, clear, 0)

            return call(
                body,
                [where, counts, tables[m]],
                [*left, *right],
                [jax.ShapeDtypeStruct((high - low, size, size), BF16) for _, low, high in spans],
                products=len(ahead) * shard,
            )

        def total(kept, arrived):
            value = kept.astype(F32)
            for g in arrived:
                value = value + g.astype(F32)
            return value.astype(BF16)[None]

        down_operands = ([*hidden, *hidden_pair], [cotangent, cotangent_pair])
        down_away = block_grads(2, away, *down_operands)
        down_far = [chip_shift(g, k, "down_grad") for g, k in zip(down_away, away)]

        relay.append(both("down_y", after(y_d, tokens_pair, *down_away)))
        acc_h = go_on(2, after(acc_h, *down_away), cotangent, direct[2], direct_keys)

        def back_body(where_ref, counts_ref, td, acc_in, c_ref, silu_ref, slope_ref, up_ref, *refs):
            outs, acc = refs[-6:-1], refs[-1]
            acc[...] = acc_in[...]
            add_pieces(acc, 2, c_ref, refs[:-6], relay_keys, td, counts_ref, where_ref)

            def finish(b, _):
                grad = acc[b]
                gate = (grad * up_ref[b] * slope_ref[b]).astype(BF16)
                up = (grad * silu_ref[b]).astype(BF16)
                for i in range(4):
                    outs[i][b] = gate[i * quarter : (i + 1) * quarter]
                outs[4][b] = up
                return 0

            lax.fori_loop(0, hidden_blocks, finish, 0)

        grads = call(
            back_body,
            [where, counts, tables[2]],
            [acc_h, cotangent, silu, slope, up_value, *relay[2]],
            [jax.ShapeDtypeStruct((hidden_blocks, quarter, size), BF16)] * 4 + [hidden_bf16],
            scratch=[pltpu.VMEM(hidden_f32.shape, F32)],
            products=shard + 10,
        )
        pieces = [near[m] + direct[m] + relay[m] for m in range(3)]

        width = model_blocks // groups
        chunk = jax.ShapeDtypeStruct((groups // 2, token_count, width * size), BF16)

        def deal(where_ref, acc, outs):
            for i in range(groups):
                to = lax.bitwise_xor(where_ref[3], i) * width
                for j in range(width):
                    outs[i % 2][i // 2, :, j * size : (j + 1) * size] = acc[to + j].astype(BF16)

        def out_body(where_ref, counts_ref, td, *refs):
            h_refs, refs = refs[:4], refs[4:]
            w_refs, outs, acc = refs[: len(every)], refs[len(every) : -1], refs[-1]
            zero(acc)
            for w_ref, key in zip(w_refs, every):
                first = place.first(where_ref, key)

                def terms(s, w_ref=w_ref, first=first):
                    h = td[1, first + s]
                    return mm(jnp.concatenate([h_ref[h] for h_ref in h_refs], axis=0), w_ref[s])

                def store(s, value, first=first):
                    acc[td[0, first + s]] += value

                over_live(live_in(counts_ref[2], first, w_ref.shape[0]), terms, store)
            deal(where_ref, acc, outs)

        model_acc = pltpu.VMEM((model_blocks, token_count, size), F32)
        out_parts = call(
            out_body,
            [where, counts, tables[2]],
            [*after(hidden, *grads), *pieces[2]],
            [chunk] * 2,
            scratch=[model_acc],
            products=4 * shard,
        )

        grads_pair = [pair_swap(g, "grads") for g in grads]
        grads_pair[:4] = after(grads_pair[:4], *out_parts)
        gate_operands = ([tokens, tokens_pair], [*grads[:4], *grads_pair[:4]])
        up_operands = ([tokens, tokens_pair], [grads[4], grads_pair[4]])
        gate_away = block_grads(0, away, *gate_operands)
        up_away = block_grads(1, away, *up_operands)
        down_far = after(down_far, *gate_away)

        def token_body(m, last, where_ref, counts_ref, table, *refs):
            n, n_y = len(all_keys[m]), 1 if m else 4
            ys, w_refs, acc = refs[:n_y], refs[n_y : n_y + n], refs[-1]
            if not last:
                zero(acc)
            for w_ref, key in zip(w_refs, all_keys[m]):
                first = place.first(where_ref, key)

                def terms(s, w_ref=w_ref, first=first):
                    h = table[1, first + s]
                    y = jnp.concatenate([y_ref[h] for y_ref in ys], axis=0)
                    return mm(y, w_ref[s], NT)

                def store(s, value, first=first):
                    acc[table[0, first + s]] += value

                over_live(live_in(counts_ref[m], first, w_ref.shape[0]), terms, store)
            if last:
                deal(where_ref, acc, refs[-3:-1])

        model_f32 = jax.ShapeDtypeStruct((model_blocks, token_count, size), F32)
        (token_acc,) = call(
            functools.partial(token_body, 0, False),
            [where, counts, tables[0]],
            [*after(grads[:4], *down_far), *pieces[0]],
            [model_f32],
            products=4 * shard,
        )
        y_up = after(grads[4], token_acc)
        *token_parts, _ = call(
            functools.partial(token_body, 1, True),
            [where, counts, tables[1]],
            [y_up, *pieces[1], token_acc],
            [chunk] * 2 + [model_f32],
            products=4 * shard,
            aliases={4 + len(pieces[1]): 2},
        )

        def swap_groups(name, chunks, *others):
            kept, sent = chunks
            bit, first = 1, None
            while True:
                arrived = group_swap(sent, bit, name)
                first = arrived if first is None else first
                bit *= 2
                if bit == groups:
                    return first, kept, arrived
                value = (kept.astype(F32) + after(arrived, *others).astype(F32)).astype(BF16)
                kept, sent = value[0::2], value[1::2]

        def last_sum(kept, arrived, *others):
            value = kept.astype(F32) + after(arrived, *others).astype(F32)
            return value[0].astype(BF16)

        gate_sent = after(gate_away, *down_far)
        gate_far = [chip_shift(g, k, "gate_grad") for g, k in zip(gate_sent, away)]
        out_first, *out_terms = swap_groups("out", out_parts, *token_parts)
        up_sent = after(up_away, out_first)
        up_far = [chip_shift(g, k, "up_grad") for g, k in zip(up_sent, away)]
        late_h, late_t = after(hidden, out_first), after(tokens, *gate_far)
        (down_kept,) = block_grads(2, (0,), [*late_h, *hidden_pair], down_operands[1])
        (gate_kept,) = block_grads(0, (0,), [late_t, tokens_pair], gate_operands[1])
        (up_kept,) = block_grads(1, (0,), [late_t, tokens_pair], up_operands[1])
        down_grad = total(down_kept, down_far)
        gate_far = after(gate_far, down_grad)
        layer_out = last_sum(*out_terms, *gate_far)
        _, *token_terms = swap_groups("token", token_parts, *gate_far)
        gate_grad = total(gate_kept, gate_far)
        token_grad = last_sum(*token_terms, layer_out, gate_grad)
        up_grad = total(up_kept, after(up_far, token_grad))
        return layer_out, token_grad, gate_grad, up_grad, down_grad

    return per_device


def solution(mesh):
    return jax.shard_map(
        make(mesh),
        mesh=mesh,
        in_specs=(
            P(("parts", "dp"), None),
            P(("parts", "dp"), None),
            P("tensor", "dp", None, None),
            P("tensor", "dp", None, None),
            P("tensor", "dp", None, None),
            P(None, "tensor", None),
            P(None, "tensor", None),
            P(None, "tensor", None),
            P(None, "tensor"),
        ),
        out_specs=(
            P(("parts", "dp"), "tensor"),
            P(("parts", "dp"), "tensor"),
            P(("parts", "tensor"), "dp", None, None),
            P(("parts", "tensor"), "dp", None, None),
            P(("parts", "tensor"), "dp", None, None),
        ),
        check_vma=False,
    )
```

```python
import functools

import jax
import jax.numpy as jnp
from jax import lax
from jax.experimental import pallas as pl
from jax.experimental.pallas import tpu as pltpu
from jax.sharding import PartitionSpec as P

FF = 14336
F32 = jnp.float32
BF16 = jnp.bfloat16
UNROLL = 7
NN = (((1,), (0,)), ((), ()))
NT = (((1,), (1,)), ((), ()))
TN = (((0,), (0,)), ((), ()))

VMEM = pl.BlockSpec(memory_space=pltpu.VMEM)
SMEM = pl.BlockSpec(memory_space=pltpu.SMEM)


def mm(left, right, dims=NN):
    return lax.dot_general(left, right, dims, preferred_element_type=F32)


def call(body, ints, arrays, outs, scratch=(), products=0, aliases=None):
    size = lambda a: a.size * a.dtype.itemsize
    total = sum(size(a) for a in arrays) + sum(size(o) for o in outs)
    held = total + sum(s.inner_aval.size * s.inner_aval.dtype.itemsize if hasattr(s, "inner_aval") else 0 for s in scratch)
    return pl.pallas_call(
        body,
        out_shape=outs,
        in_specs=[SMEM] * len(ints) + [VMEM] * len(arrays),
        out_specs=[VMEM] * len(outs),
        scratch_shapes=list(scratch),
        input_output_aliases=aliases or {},
        compiler_params=pltpu.CompilerParams(vmem_limit_bytes=held + (12 << 20)),
        cost_estimate=pl.CostEstimate(
            flops=products, bytes_accessed=products, transcendentals=0
        ),
    )(*ints, *arrays)


class Place:
    def __init__(self, chips, parts, groups, shard):
        self.chips, self.parts, self.groups, self.shard = chips, parts, groups, shard

    def first(self, where, piece):
        chip, core, part = where[0], where[1], where[2]
        back, other, half, offset = piece
        chip = lax.rem(chip + (self.chips - back), self.chips)
        core = 1 - core if other else core
        start = (chip * 2 + core) * self.shard
        if half is not None:
            start = start + (1 - part if half else part) * (self.shard // 2)
        return start + offset


def over_live(live, terms, store):
    def several(step, _):
        slots = [step * UNROLL + u for u in range(UNROLL)]
        values = [terms(slot) for slot in slots]
        for slot, value in zip(slots, values):
            store(slot, value)
        return 0

    rounds = lax.div(live, UNROLL)
    lax.fori_loop(0, rounds, several, 0)
    done = rounds * UNROLL

    @pl.when(done < live)
    def _():
        slots = [jnp.minimum(done + u, live - 1) for u in range(UNROLL - 1)]
        values = [terms(slot) for slot in slots]
        store(slots[0], values[0])
        for u in range(1, UNROLL - 1):

            @pl.when(done + u < live)
            def _(u=u):
                store(slots[u], values[u])


def live_in(count, first, extent):
    return jnp.clip(count - first, 0, extent)


def columns(block, size=128):
    return pl.ds(pl.multiple_of(block * size, size), size)


def after(value, *others):
    return lax.optimization_barrier((value, others))[0]


def zero(acc):
    acc[...] = jnp.zeros(acc.shape, acc.dtype)


def make(mesh):
    parts = mesh.shape["parts"]
    dp = mesh.shape["dp"]
    groups = mesh.shape["tensor"]
    chips = dp // 2

    def pair_swap(a, name):
        with jax.named_scope(name + "_core"):
            return lax.ppermute(a, "dp", [(i, i ^ 1) for i in range(dp)])

    def chip_shift(a, k, name):
        with jax.named_scope(name + "_chip"):
            return lax.ppermute(
                a, "dp", [(i, ((i // 2 + k) % chips) * 2 + i % 2) for i in range(dp)]
            )

    def part_swap(a, name):
        with jax.named_scope(name + "_part"):
            return lax.ppermute(a, "parts", [(0, 1), (1, 0)])

    def group_swap(a, bit, name):
        with jax.named_scope(name + "_group"):
            return lax.ppermute(a, "tensor", [(i, i ^ bit) for i in range(groups)])

    def per_device(
        tokens, cotangent, gate_blocks, up_blocks, down_blocks, gate_index, up_index, down_index, block_counts
    ):
        token_count, model_width = tokens.shape
        size = gate_blocks.shape[2]
        shard = gate_blocks.shape[1]
        model_blocks = model_width // size
        hidden_blocks = FF // size // groups
        halves = parts == 2 and shard % 2 == 0
        place = Place(chips, parts, groups, shard)
        at = lax.axis_index("dp")
        part = lax.axis_index("parts")
        where = jnp.stack([at // 2, at % 2, part, lax.axis_index("tensor")]).astype(jnp.int32)
        tables = [gate_index[:, 0], up_index[:, 0], down_index[:, 0]]
        counts = block_counts[:, 0]

        hidden_f32 = jax.ShapeDtypeStruct((hidden_blocks, token_count, size), F32)
        hidden_bf16 = jax.ShapeDtypeStruct((hidden_blocks, token_count, size), BF16)

        own = [gate_blocks[0], up_blocks[0], down_blocks[0]]
        near_keys = [(0, False, None, 0), (0, True, None, 0)]
        away = tuple(range(1, chips))
        near_half, far_half = (False, True) if halves else (None, None)
        direct_keys = [(k, other, near_half, 0) for k in away for other in (False, True)]
        relay_keys = [(k, other, far_half, 0) for k in away for other in (False, True)] if halves else []
        every = near_keys + direct_keys + relay_keys
        all_keys = [every, every, every]
        cut = own
        if halves:
            cut = [
                lax.dynamic_slice_in_dim(w, part * (shard // 2), shard // 2, 0) for w in own
            ]

        def shift_all(name, blocks, *others):
            arrived = []
            for k in away:
                arrived.append(chip_shift(after(blocks, *others), k, name))
                others = arrived[-1:]
            return arrived

        names = ("gate", "up", "down")
        near = [[w, pair_swap(w, name)] for w, name in zip(own, names)]

        def both(name, pieces):
            return [q for w in pieces for q in (w, pair_swap(w, name))]

        def add_pieces(acc, m, x_ref, w_refs, piece_keys, table, counts_ref, where_ref):
            for w_ref, key in zip(w_refs, piece_keys):
                first = place.first(where_ref, key)

                def terms(s, w_ref=w_ref, first=first):
                    return mm(x_ref[:, columns(table[0, first + s])], w_ref[s], NT if m == 2 else NN)

                def store(s, value, first=first):
                    acc[table[1, first + s]] += value

                over_live(live_in(counts_ref[m], first, w_ref.shape[0]), terms, store)

        def begin(m, x, pieces, piece_keys):
            def body(where_ref, counts_ref, table, x_ref, *refs):
                zero(refs[-1])
                add_pieces(refs[-1], m, x_ref, refs[:-1], piece_keys, table, counts_ref, where_ref)

            (acc,) = call(
                body, [where, counts, tables[m]], [x, *pieces], [hidden_f32],
                products=sum(p.shape[0] for p in pieces),
            )
            return acc

        def go_on(m, acc, x, pieces, piece_keys):
            if not pieces:
                return acc

            def body(where_ref, counts_ref, table, acc_in, x_ref, *refs):
                add_pieces(refs[-1], m, x_ref, refs[:-1], piece_keys, table, counts_ref, where_ref)

            (acc,) = call(
                body, [where, counts, tables[m]], [acc, x, *pieces], [hidden_f32],
                products=sum(p.shape[0] for p in pieces), aliases={3: 0},
            )
            return acc

        def relayed(name, pieces, *others):
            out = []
            for w in pieces if halves else []:
                out.append(part_swap(after(w, *others), name))
                others = out[-1:]
            return out

        acc_g = begin(0, tokens, near[0], near_keys)
        acc_u = begin(1, tokens, near[1], near_keys)
        tokens_pair = pair_swap(tokens, "tokens")
        cotangent_pair = pair_swap(cotangent, "cotangent")

        x_g = shift_all("gate", cut[0])
        x_g = after(x_g, acc_g, cotangent_pair)
        x_u = shift_all("up", cut[1], *x_g)
        y_g = relayed("gate", x_g)

        acc_h = begin(2, cotangent, near[2], near_keys)
        direct = [both("gate_x", after(x_g, acc_u))]
        x_u, y_g = after((x_u, y_g), acc_u, acc_h)
        x_d = shift_all("down", cut[2], *x_u)

        low = cut[1].shape[0] // 2
        sizes = (low, cut[1].shape[0] - low)
        n_fresh, n_direct = len(x_u), len(direct_keys)

        def direct_body(where_ref, counts_ref, tg, acc_in, x_ref, *refs):
            w_refs, refs = refs[:n_direct], refs[n_direct:]
            fresh, acc, outs = refs[:n_fresh], refs[n_fresh], refs[n_fresh + 1 :]
            for i, w_ref in enumerate(fresh):
                outs[2 * i][...] = w_ref[:low]
                outs[2 * i + 1][...] = w_ref[low:]
            add_pieces(acc, 0, x_ref, w_refs, direct_keys, tg, counts_ref, where_ref)

        acc_g, *split = call(
            direct_body,
            [where, counts, tables[0]],
            [acc_g, tokens, *direct[0], *x_u],
            [hidden_f32] + [jax.ShapeDtypeStruct((n, size, size), BF16) for n in sizes] * n_fresh,
            products=2 * shard,
            aliases={3: 0},
        )

        def split_swap(name, pieces, halved, half):
            blocks, its_keys = [], []
            for k, w in enumerate(pieces):
                blocks += [w] + [pair_swap(h, name) for h in halved[2 * k : 2 * k + 2]]
                its_keys += [(k + 1, other, half, o) for other, o in ((False, 0), (True, 0), (True, low))]
            return blocks, its_keys

        up_direct, up_keys = split_swap("up_x", x_u, split, near_half)
        all_keys[1] = near_keys + up_keys + relay_keys
        y_u = relayed("up", x_u)
        direct.append(up_direct)
        acc_u = go_on(1, acc_u, tokens, up_direct, up_keys)

        x_d = after(x_d, acc_u)
        y_u = after(y_u, *x_d)
        y_d = relayed("down", x_d, *y_u)
        direct.append(both("down_x", x_d))
        relay = [both("gate_y", after(y_g, acc_u)), both("up_y", y_u)]

        def gate_body(where_ref, counts_ref, tg, acc_in, x_ref, *refs):
            w_refs, silu_ref, slope_ref, acc = refs[:-3], *refs[-3:]
            acc[...] = acc_in[...]
            add_pieces(acc, 0, x_ref, w_refs, relay_keys, tg, counts_ref, where_ref)

            def finish(b, _):
                gate = acc[b]
                sigma = jax.nn.sigmoid(gate)
                silu_ref[b] = gate * sigma
                slope_ref[b] = sigma * (1.0 + gate * (1.0 - sigma))
                return 0

            lax.fori_loop(0, hidden_blocks, finish, 0)

        silu, slope = call(
            gate_body,
            [where, counts, tables[0]],
            [acc_g, tokens, *relay[0]],
            [hidden_f32, hidden_f32],
            scratch=[pltpu.VMEM(hidden_f32.shape, F32)],
            products=shard,
        )
        quarter = token_count // 4

        def up_body(where_ref, counts_ref, tu, acc_in, silu_ref, x_ref, *refs):
            w_refs, acc, h_refs = refs[:-5], refs[-5], refs[-4:]
            add_pieces(acc, 1, x_ref, w_refs, relay_keys, tu, counts_ref, where_ref)

            def finish(b, _):
                hidden = (silu_ref[b] * acc[b]).astype(BF16)
                for i, h_ref in enumerate(h_refs):
                    h_ref[b] = hidden[i * quarter : (i + 1) * quarter]
                return 0

            lax.fori_loop(0, hidden_blocks, finish, 0)

        up_value, *hidden = call(
            up_body,
            [where, counts, tables[1]],
            [acc_u, silu, tokens, *relay[1]],
            [
                hidden_f32,
                *[jax.ShapeDtypeStruct((hidden_blocks, quarter, size), BF16)] * 4,
            ],
            aliases={3: 0},
            products=shard + 20,
        )
        hidden_pair = [pair_swap(h, "hidden") for h in hidden]

        def block_grads(m, ahead, left, right, cuts=(0, shard)):
            spans = [(k, low, high) for k in ahead for low, high in zip(cuts, cuts[1:])]

            n_left, n_both = len(left), len(left) + len(right)

            def body(where_ref, counts_ref, table, *refs):
                ls, rs, outs = refs[:n_left], refs[n_left:n_both], refs[n_both:]
                for (k, low, high), o_ref in zip(spans, outs):
                    first = place.first(where_ref, ((chips - k) % chips, False, None, 0)) + low
                    live = live_in(counts_ref[m], first, high - low)

                    def terms(s, first=first):
                        f, h = table[0, first + s], table[1, first + s]
                        wide, deep = (rs, ls) if m == 2 else (ls, rs)
                        model = jnp.concatenate([ref[:, columns(f)] for ref in wide], axis=0)
                        inner = jnp.concatenate([ref[h] for ref in deep], axis=0)
                        return mm(inner, model, TN) if m == 2 else mm(model, inner, TN)

                    def store(s, value, o_ref=o_ref):
                        o_ref[s] = value.astype(BF16)

                    over_live(live, terms, store)

                    def clear(s, _, o_ref=o_ref):
                        o_ref[s] = jnp.zeros((size, size), BF16)
                        return 0

                    lax.fori_loop(live, high - low, clear, 0)

            return call(
                body,
                [where, counts, tables[m]],
                [*left, *right],
                [jax.ShapeDtypeStruct((high - low, size, size), BF16) for _, low, high in spans],
                products=len(ahead) * shard,
            )

        def total(kept, arrived):
            value = kept.astype(F32)
            for g in arrived:
                value = value + g.astype(F32)
            return value.astype(BF16)[None]

        down_operands = ([*hidden, *hidden_pair], [cotangent, cotangent_pair])
        down_away = block_grads(2, away, *down_operands)
        down_far = [chip_shift(g, k, "down_grad") for g, k in zip(down_away, away)]

        relay.append(both("down_y", after(y_d, *down_away)))
        acc_h = go_on(2, after(acc_h, *down_away), cotangent, direct[2], direct_keys)

        half_tokens = token_count // 2

        def back_body(where_ref, counts_ref, td, acc_in, c_ref, silu_ref, slope_ref, up_ref, *refs):
            outs, acc = refs[-4:-1], refs[-1]
            acc[...] = acc_in[...]
            add_pieces(acc, 2, c_ref, refs[:-4], relay_keys, td, counts_ref, where_ref)

            def finish(b, _):
                grad = acc[b]
                gate = (grad * up_ref[b] * slope_ref[b]).astype(BF16)
                up = (grad * silu_ref[b]).astype(BF16)
                for i in range(2):
                    rows = slice(i * half_tokens, (i + 1) * half_tokens)
                    outs[i][b] = gate[rows]
                outs[2][b] = up
                return 0

            lax.fori_loop(0, hidden_blocks, finish, 0)

        grads = call(
            back_body,
            [where, counts, tables[2]],
            [acc_h, cotangent, silu, slope, up_value, *relay[2]],
            [jax.ShapeDtypeStruct((hidden_blocks, half_tokens, size), BF16)] * 2 + [hidden_bf16],
            scratch=[pltpu.VMEM(hidden_f32.shape, F32)],
            products=shard + 10,
        )
        pieces = [near[m] + direct[m] + relay[m] for m in range(3)]

        width = model_blocks // groups
        chunk = jax.ShapeDtypeStruct((groups // 2, token_count, width * size), BF16)

        def deal(where_ref, acc, outs):
            for i in range(groups):
                to = lax.bitwise_xor(where_ref[3], i) * width
                for j in range(width):
                    outs[i % 2][i // 2, :, j * size : (j + 1) * size] = acc[to + j].astype(BF16)

        def out_body(where_ref, counts_ref, td, *refs):
            h_refs, refs = refs[:4], refs[4:]
            w_refs, outs, acc = refs[: len(every)], refs[len(every) : -1], refs[-1]
            zero(acc)
            for w_ref, key in zip(w_refs, every):
                first = place.first(where_ref, key)

                def terms(s, w_ref=w_ref, first=first):
                    h = td[1, first + s]
                    return mm(jnp.concatenate([h_ref[h] for h_ref in h_refs], axis=0), w_ref[s])

                def store(s, value, first=first):
                    acc[td[0, first + s]] += value

                over_live(live_in(counts_ref[2], first, w_ref.shape[0]), terms, store)
            deal(where_ref, acc, outs)

        model_acc = pltpu.VMEM((model_blocks, token_count, size), F32)
        out_parts = call(
            out_body,
            [where, counts, tables[2]],
            [*after(hidden, *grads), *pieces[2]],
            [chunk] * 2,
            scratch=[model_acc],
            products=4 * shard,
        )

        grads_pair = [pair_swap(g, "grads") for g in grads]
        grads_pair[:2] = after(grads_pair[:2], *out_parts)
        gate_operands = ([tokens, tokens_pair], [*grads[:2], *grads_pair[:2]])
        up_operands = ([tokens, tokens_pair], [grads[2], grads_pair[2]])
        gate_away = block_grads(0, away, *gate_operands)
        up_away = block_grads(1, away, *up_operands)
        down_far = after(down_far, *gate_away)

        def token_body(m, last, where_ref, counts_ref, table, *refs):
            n, n_y = len(all_keys[m]), 1 if m else 2
            ys, w_refs, acc = refs[:n_y], refs[n_y : n_y + n], refs[-1]
            if not last:
                zero(acc)
            for w_ref, key in zip(w_refs, all_keys[m]):
                first = place.first(where_ref, key)

                def terms(s, w_ref=w_ref, first=first):
                    h = table[1, first + s]
                    y = jnp.concatenate([y_ref[h] for y_ref in ys], axis=0)
                    return mm(y, w_ref[s], NT)

                def store(s, value, first=first):
                    acc[table[0, first + s]] += value

                over_live(live_in(counts_ref[m], first, w_ref.shape[0]), terms, store)
            if last:
                deal(where_ref, acc, refs[-3:-1])

        model_f32 = jax.ShapeDtypeStruct((model_blocks, token_count, size), F32)
        (token_acc,) = call(
            functools.partial(token_body, 0, False),
            [where, counts, tables[0]],
            [*after(grads[:2], *gate_away), *pieces[0]],
            [model_f32],
            products=4 * shard,
        )
        down_far = after(down_far, token_acc)
        y_up = after(grads[2], *down_far)
        *token_parts, _ = call(
            functools.partial(token_body, 1, True),
            [where, counts, tables[1]],
            [y_up, *pieces[1], token_acc],
            [chunk] * 2 + [model_f32],
            products=4 * shard,
            aliases={4 + len(pieces[1]): 2},
        )

        def swap_groups(name, chunks, *others):
            kept, sent = chunks
            bit, first = 1, None
            while True:
                arrived = group_swap(sent, bit, name)
                first = arrived if first is None else first
                bit *= 2
                if bit == groups:
                    return first, kept, arrived
                value = (kept.astype(F32) + after(arrived, *others).astype(F32)).astype(BF16)
                kept, sent = value[0::2], value[1::2]

        def last_sum(kept, arrived, *others):
            value = kept.astype(F32) + after(arrived, *others).astype(F32)
            return value[0].astype(BF16)

        gate_sent = after(gate_away, *down_far)
        gate_far = [chip_shift(g, k, "gate_grad") for g, k in zip(gate_sent, away)]
        out_first, *out_terms = swap_groups("out", after(out_parts, *gate_away), *token_parts)
        up_sent = after(up_away, out_first)
        up_far = [chip_shift(g, k, "up_grad") for g, k in zip(up_sent, away)]
        late_h, late_t = after(hidden, out_first), after(tokens, *gate_far)
        (down_kept,) = block_grads(2, (0,), [*late_h, *hidden_pair], down_operands[1])
        (gate_kept,) = block_grads(0, (0,), [late_t, tokens_pair], gate_operands[1])
        (up_kept,) = block_grads(1, (0,), [late_t, tokens_pair], up_operands[1])
        down_grad = total(down_kept, down_far)
        gate_far = after(gate_far, down_grad)
        layer_out = last_sum(*out_terms, *gate_far)
        _, *token_terms = swap_groups("token", token_parts, *gate_far)
        gate_grad = total(gate_kept, gate_far)
        token_grad = last_sum(*token_terms, layer_out, gate_grad)
        up_grad = total(up_kept, after(up_far, token_grad))
        return layer_out, token_grad, gate_grad, up_grad, down_grad

    return per_device


def solution(mesh):
    return jax.shard_map(
        make(mesh),
        mesh=mesh,
        in_specs=(
            P(("parts", "dp"), None),
            P(("parts", "dp"), None),
            P("tensor", "dp", None, None),
            P("tensor", "dp", None, None),
            P("tensor", "dp", None, None),
            P(None, "tensor", None),
            P(None, "tensor", None),
            P(None, "tensor", None),
            P(None, "tensor"),
        ),
        out_specs=(
            P(("parts", "dp"), "tensor"),
            P(("parts", "dp"), "tensor"),
            P(("parts", "tensor"), "dp", None, None),
            P(("parts", "tensor"), "dp", None, None),
            P(("parts", "tensor"), "dp", None, None),
        ),
        check_vma=False,
    )
```
